256 devices in a mesh: ctx: 64 (over z, x, core), head: 4 (over y).
Axes of the slice: x: 4, y: 4, z: 8, core: 2. Of those that a mesh axis runs over, the one named last changes fastest.
Arguments:
- x_raw: bfloat16 [16384, 4096], P('ctx', 'head'), may hold values from -30 to 30
- bc_raw: bfloat16 [16384, 256], P('ctx'), may hold values from -6 to 6
- gate_raw: bfloat16 [16384, 4096], P('ctx', 'head'), may hold values from -16 to 16
- log_decay: float32 [64, 16384], P('head', 'ctx'), may hold values from -0.8 to 0
- level_weights: float32 [16, 64, 16384], P(None, 'head', 'ctx'), may hold values from 0.25 to 2
- conv_x: float32 [4, 4096], P(None, 'head'), may hold values from -3 to 3
- conv_bc: float32 [4, 256], replicated, may hold values from -3 to 3
- norm_gain: float32 [4096], P('head'), may hold values from 0.5 to 1.5
- out_grad: bfloat16 [16384, 4096], P('ctx', 'head'), may hold values from -6 to 6
Outputs:
- layer_out: bfloat16 [16384, 4096], P('ctx', 'head')
- x_grad: bfloat16 [16384, 4096], P('ctx', 'head')
- bc_grad: bfloat16 [16384, 256], P('ctx')
The draws below stay inside these ranges and needn't reach their ends.
All inputs are finite; a program needn't handle non-finite values.
Results may differ from the reference program's by a relative error of at most 0.0013.
Values may be sent and summed in bfloat16 or wider, within the bound.
A program may use at most 128 MiB of HBM per device.

```python
import math
import jax
import jax.numpy as jnp
from jax import lax

HEADS = 64
HEAD_DIM = 64
STATE = 128
KERNEL = 4
NLEV = 16
TOK_DEV = 256
SEQ = 16384
INNER = 4096
N_CTX = 64


def draw_x_raw(key, part):
    keys = jax.random.split(key, 3)
    width = HEADS * HEAD_DIM
    noise = jax.random.normal(keys[0], (SEQ, width), jnp.float32)
    trend = jnp.arange(width, dtype=jnp.float32) / width
    column_factor = 10.0 ** (0.5 * trend + 0.5 * jax.random.uniform(keys[1], (width,), jnp.float32) - 0.52)
    row_scale = 10.0 ** (jax.random.uniform(keys[2], (SEQ, 1), jnp.float32) - 0.5)
    return jnp.clip(noise * column_factor * row_scale, -30.0, 30.0).astype(jnp.bfloat16)


def draw_gate_raw(key, part):
    keys = jax.random.split(key, 2)
    width = HEADS * HEAD_DIM
    row_scale = 10.0 ** (jax.random.uniform(keys[1], (SEQ, 1), jnp.float32) - 0.5)
    starting_amount = jax.random.normal(keys[0], (SEQ, width), jnp.float32)
    return jnp.clip(starting_amount * row_scale, -16.0, 16.0).astype(jnp.bfloat16)


def draw_log_decay(key, part):
    keys = jax.random.split(key, 8)
    order = jax.random.permutation(keys[0], HEADS)
    slow_count = HEADS // 2
    is_slow = order < slow_count
    slow_rate = jnp.exp(jax.random.uniform(keys[1], (HEADS,), jnp.float32, jnp.log(0.05 / SEQ), jnp.log(0.3 / SEQ)))
    fast_rate = jnp.exp(jax.random.uniform(keys[2], (HEADS,), jnp.float32, jnp.log(1.0 / TOK_DEV), jnp.log(1.0 / 30.0)))
    rates = jnp.where(is_slow, slow_rate, fast_rate)
    blocks = SEQ // TOK_DEV
    processor_factor = jnp.exp(jax.random.uniform(keys[3], (HEADS, blocks, 1), jnp.float32, jnp.log(0.5), jnp.log(2.0)))
    token_factor = jax.random.uniform(keys[4], (HEADS, blocks, TOK_DEV), jnp.float32, 0.5, 1.5)
    starting_amount = -(rates[:, None, None] * processor_factor * token_factor).reshape(HEADS, SEQ)
    initial_spot = jax.random.randint(keys[5], (), 0, SEQ // 2)
    latter_spot = jax.random.randint(keys[6], (), SEQ // 2, SEQ)
    objective_readings = jax.random.uniform(keys[7], (2,), jnp.float32, 0.2, 0.5)
    spot_sequence = jnp.arange(SEQ, dtype=jnp.int32)
    packet_batches = jnp.where(spot_sequence == initial_spot, jnp.log(1.0 - objective_readings[0]), 0.0)
    packet_batches = packet_batches + jnp.where(spot_sequence == latter_spot, jnp.log(1.0 - objective_readings[1]), 0.0)
    return starting_amount + packet_batches[None, :]


def shard_levels(stream_key, extent, shards, smallest, top_value):
    loudness, own = 1.0, jax.random.fold_in(stream_key, 6)
    for axis_at, parts in shards:
        draws = jnp.exp(jax.random.uniform(jax.random.fold_in(own, axis_at), (parts,), jnp.float32, smallest / len(shards), top_value / len(shards)))
        loudness = loudness * jnp.repeat(draws, extent[axis_at] // parts).reshape([-1 if axis == axis_at else 1 for axis in range(len(extent))])
    return loudness


def bell_draw(rng, extent, deviation, bound, cuts=(), held_as=jnp.bfloat16):
    entries = deviation * jax.random.normal(rng, extent, jnp.float32)
    if cuts:
        entries = entries * shard_levels(rng, extent, cuts, -0.22, 0.18)
    return jnp.clip(entries, -bound, bound).astype(held_as)


def setup_inputs(seed: int = 0) -> dict:
    splits = jax.random.split(jax.random.key(seed), 10)
    x_raw = draw_x_raw(jax.random.fold_in(splits[9], 71), 0)
    bc_raw = bell_draw(splits[1], (SEQ, 2 * STATE), 1.0, 6.0, ((0, 64),))
    gate_raw = draw_gate_raw(jax.random.fold_in(splits[9], 71), 0)
    log_decay = draw_log_decay(jax.random.fold_in(splits[9], 71), 0)
    level_weights = jnp.clip(jnp.exp(math.log(2.0) - 2.0794415 * jax.random.uniform(splits[4], (NLEV, HEADS, SEQ), jnp.float32) ** shard_levels(splits[4], (NLEV, HEADS, SEQ), ((1, 4), (2, 64)), -0.2, 0.2)), 0.25, 2.0)
    conv_x = bell_draw(splits[5], (KERNEL, INNER), KERNEL ** -0.5, 3.0, ((1, 4),), jnp.float32)
    conv_bc = bell_draw(splits[6], (KERNEL, 2 * STATE), KERNEL ** -0.5, 3.0, (), jnp.float32)
    norm_gain = jnp.clip(1.0 + 0.1 * jax.random.normal(splits[7], (INNER,), jnp.float32), 0.5, 1.5)
    out_grad = bell_draw(splits[8], (SEQ, INNER), 1.0, 6.0, ((0, 64), (1, 4)))
    return dict(x_raw=x_raw, bc_raw=bc_raw, gate_raw=gate_raw, log_decay=log_decay, level_weights=level_weights, conv_x=conv_x, conv_bc=conv_bc, norm_gain=norm_gain, out_grad=out_grad)


highest = lax.Precision.HIGHEST
epsilon = 1e-05

def bit_length(values, count):
    summed = jnp.zeros(values.shape, jnp.int32)
    for bit_pos in range(count):
        summed = summed + (values >= 2 ** bit_pos).astype(jnp.int32)
    return summed

def conv_pre(raw_rows, weights):
    tap_count = weights.shape[0]
    length = raw_rows.shape[0]
    padded = jnp.concatenate([jnp.zeros((tap_count - 1, raw_rows.shape[1]), raw_rows.dtype), raw_rows], axis=0)
    summed = jnp.zeros(raw_rows.shape, raw_rows.dtype)
    for tap_id in range(tap_count):
        summed = summed + weights[tap_id] * padded[tap_id:tap_id + length]
    return summed

def state_mixer(x_conv, b_state, c_state, log_decay, level_weights):
    width = TOK_DEV
    low_bits = width.bit_length() - 1
    ctx_bits = N_CTX.bit_length() - 1
    blocks = SEQ // width
    float_type = x_conv.dtype
    position = jnp.arange(width, dtype=jnp.int32)
    inside = bit_length(jnp.bitwise_xor(position[:, None], position[None, :]), low_bits)
    inside_all = jnp.broadcast_to(inside[None], (HEADS, width, width))
    causal = (position[:, None] >= position[None, :])[None]
    far_ids = [min(low_bits + 1 + bit_pos, NLEV - 1) for bit_pos in range(ctx_bits)]
    level_ids = jnp.arange(ctx_bits, dtype=jnp.int32)

    def block_fn(stack, inputs):
        x_block, b_block, c_block, decay_block, weight_block, block_id = inputs
        cum_decay = jnp.cumsum(decay_block, axis=1)
        block_total = cum_decay[:, -1]
        scores = jnp.dot(c_block, b_block.T, precision=highest, preferred_element_type=jnp.float32)
        near = jnp.transpose(weight_block[:low_bits + 1], (1, 2, 0))
        chosen = jnp.take_along_axis(near, inside_all, axis=2)
        exponent = jnp.where(causal, cum_decay[:, :, None] - cum_decay[:, None, :], -jnp.inf)
        mixing = chosen * jnp.exp(exponent) * scores[None]
        x_heads = x_block.reshape(width, HEADS, HEAD_DIM)
        intra = jnp.einsum('hts,shp->thp', mixing, x_heads, precision=highest).reshape(width, INNER)
        bit_flags = jnp.stack([block_id // 2 ** bit_pos % 2 for bit_pos in range(ctx_bits)]).astype(float_type)
        far_weights = jnp.stack([weight_block[far_id] for far_id in far_ids])
        far_coef = far_weights * jnp.exp(cum_decay)[None] * bit_flags[:, None, None]
        projected = jnp.einsum('tn,knm->ktm', c_block, stack, precision=highest)
        coef_wide = jnp.repeat(far_coef, HEAD_DIM, axis=1)
        inter = jnp.einsum('ktm,kmt->tm', projected, coef_wide, precision=highest)
        end_weight = jnp.repeat(jnp.exp(block_total[:, None] - cum_decay), HEAD_DIM, axis=0).T
        end_state = jnp.dot(b_block.T, x_block * end_weight, precision=highest, preferred_element_type=jnp.float32)
        run_flag = jnp.ones((), jnp.int32)
        trailing = jnp.zeros((), jnp.int32)
        for bit_pos in range(ctx_bits):
            run_flag = run_flag * (block_id // 2 ** bit_pos % 2)
            trailing = trailing + run_flag
        retain_multiplier = jnp.repeat(jnp.exp(block_total), HEAD_DIM)
        cleared = (level_ids < trailing)[:, None, None]
        lower_sum = lax.optimization_barrier(jnp.sum(jnp.where(cleared, stack, 0.0), axis=0))
        new_block = lower_sum * retain_multiplier + end_state
        stack = jnp.where(cleared, 0.0, stack * retain_multiplier)
        stack = jnp.where((level_ids == trailing)[:, None, None], new_block[None], stack)
        return (stack, intra + inter)
    inputs = (x_conv.reshape(blocks, width, INNER), b_state.reshape(blocks, width, STATE), c_state.reshape(blocks, width, STATE), jnp.transpose(log_decay.reshape(HEADS, blocks, width), (1, 0, 2)), jnp.transpose(level_weights.reshape(NLEV, HEADS, blocks, width), (2, 0, 1, 3)), jnp.arange(blocks, dtype=jnp.int32))
    empty_stack = jnp.zeros((ctx_bits, STATE, INNER), float_type)
    final_stack, outputs = lax.scan(jax.checkpoint(block_fn), empty_stack, inputs)
    return outputs.reshape(SEQ, INNER)

def layer(x_raw, bc_raw, gate_act, log_decay, level_weights, conv_x, conv_bc, norm_gain):
    x_conv = jax.nn.silu(conv_pre(x_raw, conv_x))
    bc_conv = jax.nn.silu(conv_pre(bc_raw, conv_bc))
    ssd_out = state_mixer(x_conv, bc_conv[:, :STATE], bc_conv[:, STATE:], log_decay, level_weights)
    mixed = ssd_out * gate_act
    mean_square = lax.optimization_barrier(jnp.mean(mixed * mixed, axis=1, keepdims=True))
    return norm_gain * mixed * lax.rsqrt(mean_square + epsilon)

def reference(x_raw, bc_raw, gate_raw, log_decay, level_weights, conv_x, conv_bc, norm_gain, out_grad):
    gate_act = jax.nn.silu(gate_raw.astype(jnp.float32))

    def forward(values_in, states_in):
        return layer(values_in, states_in, gate_act, log_decay, level_weights, conv_x, conv_bc, norm_gain)
    result, pullback = jax.vjp(forward, x_raw.astype(jnp.float32), bc_raw.astype(jnp.float32))
    x_grad, bc_grad = pullback(out_grad.astype(jnp.float32))
    return (result.astype(jnp.bfloat16), x_grad.astype(jnp.bfloat16), bc_grad.astype(jnp.bfloat16))
```

```python
import functools

import jax
import jax.numpy as jnp
from jax import lax
from jax.experimental import pallas as pl
from jax.experimental.pallas import tpu as pltpu
from jax.sharding import PartitionSpec as P

MESH = pl.DeviceIdType.MESH
f32 = jnp.float32
bf16 = jnp.bfloat16
L = 256
C = 1024
INNER = 4096
EPS = 1e-05
LEV = 8
DENSE = 4
WIDE = LEV - DENSE


def split(v):
    hi = v.astype(bf16)
    return hi, (v - hi.astype(f32)).astype(bf16)


def mm(a, b):
    return jnp.dot(a, b, preferred_element_type=f32)


def mt(a, b):
    return lax.dot_general(a, b, (((1,), (1,)), ((), ())), preferred_element_type=f32)


def cat(parts, axis):
    return jnp.concatenate(parts, axis=axis)


def mm3(ah, al, bh, bl):
    return mm(cat([ah, ah, al], 1), cat([bh, bl, bh], 0))


def mt3(ah, al, bh, bl):
    return mt(cat([ah, ah, al], 1), cat([bh, bl, bh], 1))


def loop(n, fn, unroll=1):
    def step(i, carry):
        for t in range(unroll):
            fn(i * unroll + t)
        return carry

    lax.fori_loop(0, n // unroll, step, 0)


def sigmoid(v):
    return 1.0 / (1.0 + jnp.exp(-v))


def kernel(
    Z, Y, names,
    x_ref, bc_ref, gate_ref, og_ref, ld_ref, lw_ref, tx_ref, tb_ref, gain_ref,
    out_ref, xg_ref, bg_ref, *scratch,
):
    r = dict(zip(names, scratch))
    nz = Z.bit_length() - 1
    nctx = Z * 8
    nf = 3 + nz
    ctx = lax.axis_index("ctx")
    hd = lax.axis_index("head")
    core = ctx % 2
    xx = (ctx // 2) % 4
    zz = ctx // 8
    core_f = core.astype(f32)
    ssem, rsem = r["ssem"], r["rsem"]
    ids = {}

    def rc(key, src, dst, dev):
        i = ids.setdefault(key, len(ids))
        return pltpu.make_async_remote_copy(
            src_ref=src, dst_ref=dst, send_sem=ssem.at[i], recv_sem=rsem.at[i],
            device_id=dev, device_id_type=MESH,
        )

    def at_x(q):
        return (zz * 8 + q * 2 + core, hd)

    def mirror(m):
        w = 2 ** (m + 1)
        return ((zz // w) * w + (w - 1) - zz % w) * 8 + xx * 2 + core

    def zbit(m):
        return (zz // 2**m) % 2

    other = (ctx + 1 - 2 * core, hd)
    following = ((ctx + 1) % nctx, hd)
    preceding = ((ctx + nctx - 1) % nctx, hd)

    def cbit(l):
        if l == 1:
            return xx % 2
        if l == 2:
            return xx // 2
        return zbit(l - 3)

    peers = [other, following, preceding]
    peers += [at_x((xx + d) % 4) for d in (1, 2, 3)]
    peers += [(mirror(m), hd) for m in range(nz)]
    peers += [(ctx, (hd + d) % Y) for d in range(1, Y)]
    yp = []
    w = 2
    while w <= Y:
        yp.append((ctx, (hd // w) * w + (w - 1) - hd % w))
        w *= 2
    barrier = pltpu.get_barrier_semaphore()
    for dev in peers:
        pl.semaphore_signal(barrier, inc=1, device_id=dev, device_id_type=MESH)

    pend = []

    def cols(j):
        return pl.ds(pl.multiple_of(j * 256, 256), 256)

    row = lax.broadcasted_iota(jnp.int32, (L, L), 0)
    col = lax.broadcasted_iota(jnp.int32, (L, L), 1)
    dist = row ^ col
    r["zle"][...] = jnp.where(row <= col, dist, 4096)
    r["zgt"][...] = jnp.where(row > col, dist, 4096)
    r["zlt"][...] = jnp.where(row < col, dist, 4096)

    def make_ex(o):
        a = lax.broadcasted_iota(jnp.int32, (L, L), 0) % 128
        b = lax.broadcasted_iota(jnp.int32, (L, L), 1) // 64
        r["ex"][o] = jnp.where(a == b + 4 * o, 1.0, 0.0).astype(bf16)

    loop(32, make_ex)
    pl.semaphore_wait(barrier, len(peers))
    hx = rc("hx", x_ref.at[L - 16 : L], r["hx"], following)
    hb = rc("hb", bc_ref.at[L - 16 : L], r["hb"], following)
    hx.start()
    hb.start()
    pend += [hx, hb]
    ld = ld_ref[...]
    l0 = ld.astype(bf16)
    rest = ld - l0.astype(f32)
    l1 = rest.astype(bf16)
    l2 = (rest - l1.astype(f32)).astype(bf16)
    r["ld"][...] = cat([l0, l1, l2], 0)
    q = r["q"]

    def sums(mask):
        t = mm(r["ld"][...], jnp.where(mask, 1.0, 0.0).astype(bf16))
        return t[0:16] + t[16:32] + t[32:48]

    def coefs(k):
        th = lax.shift_left(jnp.int32(1), k)
        up = sums(r["zle"][...] < th)
        dn = sums(r["zgt"][...] < th)
        at = pl.ds(pl.multiple_of(k * 16, 16), 16)
        q[0, at, :] = lw_ref[k + 1] * jnp.exp(up)
        q[1, at, :] = jnp.exp(dn)

    loop(LEV, coefs)
    up = sums(r["zle"][...] < L)
    dn = sums(r["zgt"][...] < L)
    eup = jnp.exp(up)
    for l in range(nf):
        q[2, l * 16 : l * 16 + 16, :] = lw_ref[min(LEV + 1 + l, 15)] * eup
    for l in range(nf, 6):
        q[2, l * 16 : l * 16 + 16, :] = jnp.zeros((16, L), f32)
    q[2, 96:112, :] = jnp.exp(dn)
    q[2, 112:128, :] = jnp.broadcast_to(eup[:, L - 1 : L], (16, L))
    q[3] = jnp.zeros((128, L), f32)
    q[3, 0:16, :] = lw_ref[0]
    for g in range(4):
        hi, lo = split(q[g].T)
        r["qt"][g, :, 0:128] = hi
        r["qt"][g, :, 128:256] = lo

    def spread(g, i, j):
        return mm(r["qt"][g], r["ex"][i * 4 + j])

    xp, bp = r["xp"], r["bp"]

    def widen(j):
        xp[j, 8 : L + 8, :] = x_ref[:, cols(j)].astype(f32)

    loop(4, widen)
    bp[8 : L + 8, :] = bc_ref[...].astype(f32)
    has_prev = jnp.where(ctx > 0, 1.0, 0.0).astype(f32)
    hx.wait_recv()
    hb.wait_recv()
    for j in range(4):
        xp[j, 0:8, :] = r["hx"][:, j * 256 : j * 256 + 256].astype(f32)[8:16] * has_prev
    bp[0:8, :] = r["hb"][...].astype(f32)[8:16] * has_prev

    bpre = tb_ref[0:1] * bp[5 : L + 5, :]
    for k in range(1, 4):
        bpre = bpre + tb_ref[k : k + 1] * bp[5 + k : L + 5 + k, :]
    bsig = sigmoid(bpre)
    r["bslope"][...] = bsig * (1.0 + bpre * (1.0 - bsig))
    nbs = rc("nbs", r["bslope"].at[0:8], r["nbs"], preceding)
    nbs.start()
    pend.append(nbs)
    bcv = bpre * bsig
    r["bcv"][...] = bcv
    b = bcv[:, 0:128]
    c = bcv[:, 128:256]
    bh, bl = split(b)
    ch, cl = split(c)
    bth, btl = split(b.T)
    cth, ctl = split(c.T)
    r["b2"][...] = cat([bh, bl], 1)
    r["c2"][...] = cat([ch, cl], 1)
    r["bt3"][...] = cat([bth, bth, btl], 1)
    r["ct3"][...] = cat([cth, cth, ctl], 1)
    pst = r["pst"]

    def conv(j):
        pre = tx_ref[0:1, cols(j)] * xp[j, 5 : L + 5, :]
        for k in range(1, 4):
            pre = pre + tx_ref[k : k + 1, cols(j)] * xp[j, 5 + k : L + 5 + k, :]
        sig = sigmoid(pre)
        x = pre * sig
        r["x"][j] = x
        r["slope"][j] = sig * (1.0 + pre * (1.0 - sig))
        hi, lo = split(x * spread(2, 6, j))
        r["xend"][j, 0:L] = hi
        r["xend"][j, L : 2 * L] = lo
        s = mm(r["bt3"][...], cat([hi, lo, hi], 0))
        d = mm(r["qt"][2, 0:16, :], r["ex"][28 + j])[0:8]
        for h in range(2):
            pst[2 * j + h, 0:128] = s[:, h * 128 : h * 128 + 128]
            pst[2 * j + h, 128:136] = d[:, h * 128 : h * 128 + 128]

    loop(4, conv)

    p0 = rc("p0", pst, r["poth"], other)
    p0.start()
    pend.append(p0)
    poth = r["poth"]

    sc = mt3(ch, cl, bh, bl)
    sct = mt3(bh, bl, ch, cl)
    r["sc"][...] = sc
    r["sct"][...] = sct
    diag = jnp.sum(c * b, axis=1, keepdims=True)
    r["diag"][...] = jnp.broadcast_to(diag, (L, 128))

    def level_masks(k):
        th = lax.shift_left(jnp.int32(1), k)
        z = r["zgt"][...]
        hi, lo = split(jnp.where((z >= th) & (z < 2 * th), r["sc"][...], 0.0))
        r["sm"][k, :, 0:L] = hi
        r["sm"][k, :, L : 2 * L] = lo
        z = r["zlt"][...]
        hi, lo = split(jnp.where((z >= th) & (z < 2 * th), r["sct"][...], 0.0))
        r["smt"][k, :, 0:L] = hi
        r["smt"][k, :, L : 2 * L] = lo

    loop(DENSE, level_masks)

    def low(k, get):
        h = 2**k
        return cat([get(s, s + h) for s in range(0, L, 2 * h)], 0)

    def upp(k, get):
        h = 2**k
        return cat([get(s + h, s + 2 * h) for s in range(0, L, 2 * h)], 0)

    def same(k):
        u = lax.broadcasted_iota(jnp.int32, (128, 128), 0) // 2**k
        v = lax.broadcasted_iota(jnp.int32, (128, 128), 1) // 2**k
        return u == v

    for k in range(DENSE, LEV):
        cu = upp(k, lambda a, b: r["c2"][a:b])
        bw = low(k, lambda a, b: r["b2"][a:b])
        cuh, cul, bwh, bwl = cu[:, 0:128], cu[:, 128:256], bw[:, 0:128], bw[:, 128:256]
        w = k - DENSE
        hi, lo = split(jnp.where(same(k), mt3(cuh, cul, bwh, bwl), 0.0))
        r["wm"][w, :, 0:128] = hi
        r["wm"][w, :, 128:256] = lo
        hi, lo = split(jnp.where(same(k), mt3(bwh, bwl, cuh, cul), 0.0))
        r["wmt"][w, :, 0:128] = hi
        r["wmt"][w, :, 128:256] = lo

    def near(j):
        dg = r["diag"][...]
        r["acc"][j] = spread(3, 0, j) * (cat([dg, dg], 1) * r["x"][j])

        def level(k):
            e = spread(1, k, j)
            r["ef"][k, j] = e
            hi, lo = split(r["x"][j] * e)
            r["xe"][k, j, 0:L] = hi
            r["xe"][k, j, L : 2 * L] = lo
            m = r["sm"][k]
            y = mm(cat([m[:, 0:L], m], 1), cat([hi, lo, hi], 0))
            a = spread(0, k, j)
            r["acc"][j] = r["acc"][j] + a * y

        loop(DENSE, level, 2)
        for k in range(DENSE, LEV):
            w, h = k - DENSE, 2**k
            e = mm(low(k, lambda a, b: r["qt"][1, a:b]), r["ex"][k * 4 + j])
            r["we"][w, j] = e
            hi, lo = split(low(k, lambda a, b: r["x"][j, a:b]) * e)
            r["wx"][w, j, 0:128] = hi
            r["wx"][w, j, 128:256] = lo
            m = r["wm"][w]
            y = mm(cat([m[:, 0:128], m], 1), cat([hi, lo, hi], 0))
            a = mm(upp(k, lambda a, b: r["qt"][0, a:b]), r["ex"][k * 4 + j])
            r["wa"][w, j] = a
            y = y * a
            for i in range(128 // h):
                at = slice((2 * i + 1) * h, (2 * i + 2) * h)
                r["acc"][j, at] = r["acc"][j, at] + y[i * h : (i + 1) * h]

    p0.wait_recv()
    ps, xr, ff = r["ps"], r["xr"], r["ff"]
    for h in range(4):
        own = pst[core * 4 + h]
        oth = poth[core * 4 + h]
        lo = jnp.where(core == 0, own, oth)
        hi = jnp.where(core == 0, oth, own)
        ps[h, 0:128] = lo[0:128] * hi[128:129] + hi[0:128]
        ps[h, 128:136] = lo[128:136] * hi[128:136]
    xr[xx] = ps[xx]
    for p in range(8):
        dd = poth[p, 128:136]
        r["cf"][p] = jnp.where(core == 1, dd, 1.0)
        r["df"][p] = jnp.where(core == 0, dd, 1.0)
    xs = []
    for d in (1, 2, 3):
        to = (xx + d) % 4
        xs.append(rc(("xs", d), ps.at[to], xr.at[xx], at_x(to)))
        xs[-1].start()
    pend += xs

    near(0)

    for cp in xs:
        cp.wait_recv()
    dec = [xr[i, 128:129] for i in range(4)]
    b01 = xr[0, 0:128] * dec[1] + xr[1, 0:128]
    b23 = xr[2, 0:128] * dec[3] + xr[3, 0:128]
    d01 = dec[0] * dec[1]
    d23 = dec[2] * dec[3]
    zs, zr, fb, bx, befs = r["zs"], r["zr"], r["fb"], r["bx"], r["befs"]
    zs[0, 0:128] = b01 * d23 + b23
    zs[0, 128:136] = jnp.broadcast_to(d01 * d23, (8, 128))
    fb[0] = b01
    fb[1] = b01 * dec[2]
    bx[0] = jnp.ones((8, 128), f32)
    bx[1] = jnp.broadcast_to(dec[0], (8, 128))
    bx[2] = jnp.broadcast_to(d01, (8, 128))
    bx[3] = jnp.broadcast_to(d01 * dec[2], (8, 128))
    befs[0] = jnp.ones((8, 128), f32)

    def z_copy(m):
        return rc(("z", m), zs.at[m], zr.at[m], (mirror(m), hd))

    def z_start(m):
        if m < nz - 1:
            z_copy(m).start()
        else:
            @pl.when(zbit(m) == 0)
            def _():
                z_copy(m).start()

    def f_copy(l, d):
        to = (xx + d) % 4
        if l == 1:
            src = xr.at[(to + 3) % 4, 0:128]
        elif l == 2:
            src = fb.at[to % 2]
        else:
            src = r["fst"].at[l - 3, to]
        return rc(("f", l, d), src, ff.at[l - 1, core, xx], at_x(to))

    def to_bit(l, d):
        to = (xx + d) % 4
        return to % 2 if l == 1 else to // 2 if l == 2 else zbit(l - 3)

    def from_bit(l, d):
        fr = (xx + 4 - d) % 4
        return fr % 2 if l == 1 else fr // 2 if l == 2 else zbit(l - 3)

    def f_send(l):
        for d in (1, 2, 3):
            @pl.when(to_bit(l, d) == 1)
            def _():
                f_copy(l, d).start()

    def fo_copy(l):
        return rc(("fo", l), ff.at[l - 1, core], ff.at[l - 1, core], other)

    def f_relay(l):
        @pl.when(cbit(l) == 1)
        def _():
            for d in (1, 2, 3):
                f_copy(l, d).wait_recv()
            fo_copy(l).start()

    z_start(0)

    @pl.when(xx % 2 == 1)
    def _():
        ff[0, core, xx] = xr[(xx + 3) % 4, 0:128]

    @pl.when(xx // 2 == 1)
    def _():
        ff[1, core, xx] = fb[xx % 2]

    f_send(2)
    f_send(1)

    def z_done(m):
        up = zbit(m)

        @pl.when(up == 1)
        def _():
            z_copy(m).wait_recv()
            f = zr[m, 0:128] * befs[m, 0:1]
            for i in range(4):
                r["fst"][m, i] = f * bx[i, 0:1]
            ff[2 + m, core, xx] = f * bx[xx, 0:1]
            if m < nz - 1:
                zs[m + 1, 0:128] = zr[m, 0:128] * zs[m, 128:129] + zs[m, 0:128]
                befs[m + 1] = befs[m] * zr[m, 128:136]

        if m < nz - 1:
            @pl.when(up == 0)
            def _():
                z_copy(m).wait_recv()
                zs[m + 1, 0:128] = zs[m, 0:128] * zr[m, 128:129] + zr[m, 0:128]
                befs[m + 1] = befs[m]

            zs[m + 1, 128:136] = zs[m, 128:136] * zr[m, 128:136]
            z_start(m + 1)
        f_send(3 + m)

    near(1)
    z_done(0)
    f_relay(2)
    f_relay(1)
    near(2)
    if nz > 1:
        z_done(1)
    f_relay(3)
    near(3)

    fhl = r["fhl"]

    def inter(l, j, f):
        hi, lo = split(f)
        fhl[l, j, 0:128] = hi
        fhl[l, j, 128:256] = lo
        c2 = r["c2"][...]
        y = mm(cat([c2[:, 0:128], c2[:, 0:128]], 1), cat([hi, lo], 0)) + mm(c2[:, 128:256], hi)
        r["acc"][j] = r["acc"][j] + spread(2, l, j) * y

    @pl.when(core == 1)
    def _():
        def f0(j):
            inter(0, j, cat([poth[2 * j, 0:128], poth[2 * j + 1, 0:128]], 1))

        loop(4, f0)

    def far(l):
        @pl.when(cbit(l) == 1)
        def _():
            fo_copy(l).wait_recv()

            def one(j):
                parts = [
                    ff[l - 1, j // 2, (j % 2) * 2 + h] * r["cf"][2 * j + h, 0:1] for h in range(2)
                ]
                inter(l, j, cat(parts, 1))

            loop(4, one, 2)

    far(2)
    far(1)
    for m in range(2, nz):
        z_done(m)
        if m == 2:
            f_relay(4)
    far(3)
    for l in range(4, nf):
        if l > 4 or nz <= 2:
            f_relay(l)
        far(l)

    r["st"][...] = jnp.zeros((2, L, 128), f32)

    def gated(j):
        g = gate_ref[:, cols(j)].astype(f32)
        ga = g * sigmoid(g)
        r["gact"][j] = ga
        mixed = r["acc"][j] * ga
        r["acc"][j] = mixed
        sg = gain_ref[:, cols(j)] * og_ref[:, cols(j)].astype(f32)
        r["g"][j] = sg
        sq = mixed * mixed
        cr = sg * mixed
        r["st"][0] = r["st"][0] + (sq[:, 0:128] + sq[:, 128:256])
        r["st"][1] = r["st"][1] + (cr[:, 0:128] + cr[:, 128:256])

    loop(4, gated)
    s0 = jnp.sum(r["st"][0], axis=1, keepdims=True)
    s1 = jnp.sum(r["st"][1], axis=1, keepdims=True)
    lane = lax.broadcasted_iota(jnp.int32, (L, 128), 1)
    both = jnp.where(lane == 0, s0, s1)
    r["sts"][...] = both.T[0:8]
    ys = []
    for d in range(1, Y):
        ys.append(rc(("st", d), r["sts"], r["str"].at[d - 1], (ctx, (hd + d) % Y)))
        ys[-1].start()
    pend += ys
    tot = r["sts"][...]
    for d in range(1, Y):
        ys[d - 1].wait_recv()
        tot = tot + r["str"][d - 1]
    inv_row = lax.rsqrt(tot[0:1] / INNER + EPS)
    k_row = inv_row * inv_row * inv_row * (tot[1:2] / INNER)
    r["inv"][...] = jnp.broadcast_to(inv_row, (128, L)).T
    r["kk"][...] = jnp.broadcast_to(k_row, (128, L)).T

    def normed(j):
        inv = cat([r["inv"][...]] * 2, 1)
        kk = cat([r["kk"][...]] * 2, 1)
        mixed = r["acc"][j]
        out_ref[:, cols(j)] = (gain_ref[:, cols(j)] * mixed * inv).astype(bf16)
        r["g"][j] = (r["g"][j] * inv - mixed * kk) * r["gact"][j]

    loop(4, normed)

    gf, go, ga_, gx = r["gf"], r["go"], r["ga"], r["gx"]

    def go_copy(l):
        return rc(("go", l), gf.at[l, pl.ds((1 - core) * 4, 4)], go.at[l - 1], other)

    def far_grad(l):
        def one(j):
            hi, lo = split(r["g"][j] * spread(2, l, j))
            s = mm(r["ct3"][...], cat([hi, lo, hi], 0))
            r["cg"][...] = r["cg"][...] + mt3(hi, lo, fhl[l, j, 0:128], fhl[l, j, 128:256])
            for h in range(2):
                piece = s[:, h * 128 : h * 128 + 128]
                if l > 0:
                    piece = piece * r["cf"][2 * j + h, 0:1]
                gf[l, 2 * j + h] = piece

        loop(4, one, 2)

    def g0_copy():
        return rc("g0", gf.at[0], r["g0r"], other)

    def gx_copy(l, d):
        to = (xx + d) % 4
        return rc(("gx", l, d), ga_.at[l - 1, to], gx.at[l - 1, xx], at_x(to))

    def g_pair(l):
        @pl.when(cbit(l) == 1)
        def _():
            go_copy(l).wait_recv()
            for h in range(4):
                ga_[l - 1, h] = gf[l, core * 4 + h] + go[l - 1, h]
            for d in (1, 2, 3):
                gx_copy(l, d).start()
            gx[l - 1, xx] = ga_[l - 1, xx]

    def fg(l):
        @pl.when((core if l == 0 else cbit(l)) == 1)
        def _():
            far_grad(l)
            (go_copy(l) if l else g0_copy()).start()

    r["ds"][...] = jnp.zeros((L, L), f32)
    r["cg"][...] = jnp.zeros((L, 128), f32)
    r["bgw"][...] = jnp.zeros((L, 128), f32)

    fg(nf - 1)
    for l in range(nf - 2, -1, -1):
        fg(l)
        g_pair(l + 1)

    def first_dx(j):
        dg = r["diag"][...]
        gw = r["g"][j] * spread(3, 0, j)
        r["dx"][j] = gw * cat([dg, dg], 1)
        pr = gw * r["x"][j]
        r["dv"][...] = r["dv"][...] + (pr[:, 0:128] + pr[:, 128:256])

    r["dv"][...] = jnp.zeros((L, 128), f32)
    loop(4, first_dx)

    def near_ds(k):
        r["dsk"][...] = jnp.zeros((L, L), f32)

        def one(j):
            hi, lo = split(r["g"][j] * spread(0, k, j))
            r["ga2"][k, j, 0:L] = hi
            r["ga2"][k, j, L : 2 * L] = lo
            eh = r["xe"][k, j, 0:L]
            el = r["xe"][k, j, L : 2 * L]
            r["dsk"][...] = r["dsk"][...] + mt3(hi, lo, eh, el)

        loop(4, one, 2)
        th = lax.shift_left(jnp.int32(1), k)
        z = r["zgt"][...]
        r["ds"][...] = r["ds"][...] + jnp.where((z >= th) & (z < 2 * th), r["dsk"][...], 0.0)

    def near_dx(k):
        def one(j):
            hi = r["ga2"][k, j, 0:L]
            lo = r["ga2"][k, j, L : 2 * L]
            m = r["smt"][k]
            y = mm(cat([m[:, 0:L], m], 1), cat([hi, lo, hi], 0))
            r["dx"][j] = r["dx"][j] + r["ef"][k, j] * y

        loop(4, one, 2)

    def wide_ds(k):
        w, h = k - DENSE, 2**k
        r["wds"][...] = jnp.zeros((128, 128), f32)

        def one(j):
            hi, lo = split(upp(k, lambda a, b: r["g"][j, a:b]) * r["wa"][w, j])
            r["wg"][w, j, 0:128] = hi
            r["wg"][w, j, 128:256] = lo
            eh = r["wx"][w, j, 0:128]
            el = r["wx"][w, j, 128:256]
            r["wds"][...] = r["wds"][...] + mt3(hi, lo, eh, el)

        loop(4, one, 2)
        d = jnp.where(same(k), r["wds"][...], 0.0)
        dh, dl = split(d)
        th, tl = split(d.T)
        cu = upp(k, lambda a, b: r["c2"][a:b])
        bw = low(k, lambda a, b: r["b2"][a:b])
        cg = mm3(dh, dl, bw[:, 0:128], bw[:, 128:256])
        bg = mm3(th, tl, cu[:, 0:128], cu[:, 128:256])
        for i in range(128 // h):
            at = slice(2 * i * h, (2 * i + 1) * h)
            r["bgw"][at] = r["bgw"][at] + bg[i * h : (i + 1) * h]
            at = slice((2 * i + 1) * h, (2 * i + 2) * h)
            r["cg"][at] = r["cg"][at] + cg[i * h : (i + 1) * h]

    def wide_dx(k):
        w, h = k - DENSE, 2**k

        def one(j):
            hi = r["wg"][w, j, 0:128]
            lo = r["wg"][w, j, 128:256]
            m = r["wmt"][w]
            y = mm(cat([m[:, 0:128], m], 1), cat([hi, lo, hi], 0)) * r["we"][w, j]
            for i in range(128 // h):
                at = slice(2 * i * h, (2 * i + 1) * h)
                r["dx"][j, at] = r["dx"][j, at] + y[i * h : (i + 1) * h]

        loop(4, one, 2)

    def dense(fn, lo, hi):
        def step(k, carry):
            fn(k)
            return carry

        lax.fori_loop(lo, hi, step, 0)

    dzs, dzr, dcur = r["dzs"], r["dzr"], r["dcur"]

    def dz_copy(m):
        return rc(("dz", m), dzs.at[m], dzr.at[m], (mirror(m), hd))

    def dz_start(m):
        last = m == nz - 1

        @pl.when(zbit(m) == 1)
        def _():
            for d in (1, 2, 3):
                gx_copy(3 + m, d).wait_recv()
            f = gx[2 + m, 0]
            for i in range(1, 4):
                f = f + gx[2 + m, i] * bx[i, 0:1]
            f = f * befs[m, 0:1]
            if not last:
                f = f + dcur[...] * zs[m, 128:129]
            dzs[m] = f
            dz_copy(m).start()

        if not last:
            @pl.when(zbit(m) == 0)
            def _():
                dzs[m] = dcur[...]
                dz_copy(m).start()

    def dz_done(m):
        if m == nz - 1:
            @pl.when(zbit(m) == 1)
            def _():
                dcur[...] = jnp.zeros((128, 128), f32)

            @pl.when(zbit(m) == 0)
            def _():
                dz_copy(m).wait_recv()
                dcur[...] = dzr[m]
        else:
            dz_copy(m).wait_recv()

            @pl.when(zbit(m) == 1)
            def _():
                dcur[...] = dcur[...] + dzr[m]

            @pl.when(zbit(m) == 0)
            def _():
                dcur[...] = dcur[...] * zr[m, 128:129] + dzr[m]

    dz_start(nz - 1)
    dense(near_ds, 0, DENSE)
    for k in range(DENSE, LEV):
        wide_ds(k)
        if k == DENSE + 1 and nz > 1:
            dz_done(nz - 1)
            dz_start(nz - 2)
    if nz == 1:
        dz_done(0)
    ds = r["ds"][...]
    dsh, dsl = split(ds)
    dth, dtl = split(ds.T)
    b2 = r["b2"][...]
    c2 = r["c2"][...]
    dv = jnp.sum(r["dv"][...], axis=1, keepdims=True)
    cg = r["cg"][...] + mm3(dsh, dsl, b2[:, 0:128], b2[:, 128:256]) + dv * r["bcv"][:, 0:128]
    bg = r["bgw"][...] + mm3(dth, dtl, c2[:, 0:128], c2[:, 128:256]) + dv * r["bcv"][:, 128:256]
    r["bce"][0, :, 0:128] = bg
    r["bce"][0, :, 128:256] = cg
    def y_start(key, src, dst, step):
        cp = rc((key, step), src.at[step], dst.at[step], yp[step])
        cp.start()
        pend.append(cp)
        return cp

    def y_sum(key, src, dst, step):
        rc((key, step), src.at[step], dst.at[step], yp[step]).wait_recv()
        src[step + 1] = src[step] + dst[step]

    ny = len(yp)
    if ny:
        y_start("be", r["bce"], r["bcer"], 0)

    for m in range(nz - 2, -1, -1):
        dz_done(m)
        if m:
            dz_start(m - 1)
        if m == nz - 2:
            dense(near_dx, 0, 2)

    dps, dph = r["dps"], r["dph"]
    for l in (1, 2):
        for d in (1, 2, 3):
            @pl.when(from_bit(l, d) == 1)
            def _():
                gx_copy(l, d).wait_recv()

    dt = dcur[...]
    dec = [xr[i, 128:129] for i in range(4)]
    d01 = dt * (dec[2] * dec[3]) + (gx[1, 2] + gx[1, 3] * dec[2])
    dps[0] = d01 * dec[1] + gx[0, 1]
    dps[1] = d01
    dps[2] = dt * dec[3] + gx[0, 3]
    dps[3] = dt
    dpc = []
    for d in (1, 2, 3):
        to = (xx + d) % 4
        dpc.append(rc(("dp", d), dps.at[to], dph.at[core * 4 + xx], at_x(to)))
        dpc[-1].start()
    pend += dpc
    dph[core * 4 + xx] = dps[xx]

    dense(near_dx, 2 if nz > 1 else 0, DENSE)
    for k in range(DENSE, LEV):
        wide_dx(k)

    for cp in dpc:
        cp.wait_recv()
    half = pl.ds(core * 4, 4)
    dpo = rc("dpo", dph.at[half], dph.at[half], other)
    dpo.start()

    dpo.wait()

    @pl.when(core == 0)
    def _():
        g0_copy().wait_recv()
        for p in range(8):
            dph[p] = dph[p] * r["df"][p, 0:1] + r["g0r"][p]

    r["bl"][0] = jnp.zeros((L, 128), f32)
    xsl = r["xp"]

    def last_dx(j):
        hi, lo = split(cat([dph[2 * j], dph[2 * j + 1]], 1))
        r["bl"][0] = r["bl"][0] + mt3(r["xend"][j, 0:L], r["xend"][j, L : 2 * L], hi, lo)
        b2 = r["b2"][...]
        y = mm(cat([b2[:, 0:128], b2[:, 0:128]], 1), cat([hi, lo], 0)) + mm(b2[:, 128:256], hi)
        dx = r["dx"][j] + spread(2, 6, j) * y
        sl = dx * r["slope"][j]
        xsl[j, 0:L] = sl
        r["hxs"][:, cols(j)] = sl[0:8]

    loop(4, last_dx)
    nx = rc("nx", r["hxs"], r["hxr"], preceding)
    nx.start()
    n8 = rc("n8", r["bl"].at[0, 0:8], r["bs"].at[0], preceding)
    n8.start()
    pend += [nx, n8]
    if ny:
        y_start("bl", r["bl"], r["blr"], 0)
    for i in range(ny):
        y_sum("be", r["bce"], r["bcer"], i)
        if i < ny - 1:
            y_start("be", r["bce"], r["bcer"], i + 1)
    n8.wait_recv()
    if ny:
        y_start("bs", r["bs"], r["bsr"], 0)
    nbe = rc("nbe", r["bce"].at[ny, 0:8], r["nbe"], preceding)
    nbe.start()
    pend.append(nbe)
    has_next = jnp.where(ctx < nctx - 1, 1.0, 0.0).astype(f32)

    nx.wait_recv()
    for j in range(4):
        xsl[j, L : L + 8] = r["hxr"][:, j * 256 : j * 256 + 256] * has_next

    def conv_back(j):
        v = tx_ref[3:4, cols(j)] * xsl[j, 0:L]
        for k in range(3):
            v = v + tx_ref[k : k + 1, cols(j)] * xsl[j, 3 - k : L + 3 - k]
        xg_ref[:, cols(j)] = v.astype(bf16)

    loop(4, conv_back)
    for i in range(ny):
        y_sum("bl", r["bl"], r["blr"], i)
        y_sum("bs", r["bs"], r["bsr"], i)
        if i < ny - 1:
            y_start("bl", r["bl"], r["blr"], i + 1)
            y_start("bs", r["bs"], r["bsr"], i + 1)
    total = r["bce"][ny]
    bp[0:L, :] = cat([total[:, 0:128] + r["bl"][ny], total[:, 128:256]], 1) * r["bslope"][...]
    nbs.wait_recv()
    nbe.wait_recv()
    total = r["nbe"][...]
    rows = cat([total[:, 0:128] + r["bs"][ny], total[:, 128:256]], 1)
    bp[L : L + 8, :] = rows * r["nbs"][...] * has_next
    v = tb_ref[3:4] * bp[0:L, :]
    for k in range(3):
        v = v + tb_ref[k : k + 1] * bp[3 - k : L + 3 - k, :]
    bg_ref[...] = v.astype(bf16)

    for cp in pend:
        cp.wait_send()
    for m in range(nz):
        if m < nz - 1:
            z_copy(m).wait_send()
            dz_copy(m).wait_send()
        else:
            @pl.when(zbit(m) == 0)
            def _():
                z_copy(m).wait_send()

            @pl.when(zbit(m) == 1)
            def _():
                dz_copy(m).wait_send()
    for l in range(1, nf):
        for d in (1, 2, 3):
            @pl.when(to_bit(l, d) == 1)
            def _():
                f_copy(l, d).wait_send()

        @pl.when(cbit(l) == 1)
        def _():
            fo_copy(l).wait_send()
            go_copy(l).wait_send()
            for d in (1, 2, 3):
                gx_copy(l, d).wait_send()

    @pl.when(core == 1)
    def _():
        g0_copy().wait_send()


def solution(mesh):
    nctx, Y = mesh.shape["ctx"], mesh.shape["head"]
    Z = nctx // 8
    nz = Z.bit_length() - 1
    nf = 3 + nz
    ny = Y.bit_length() - 1
    V = pltpu.VMEM
    shapes = dict(
        zle=V((L, L), jnp.int32), zgt=V((L, L), jnp.int32), zlt=V((L, L), jnp.int32),
        ex=V((32, L, L), bf16), ld=V((48, L), bf16), q=V((4, 128, L), f32), qt=V((4, L, L), bf16),
        hx=V((16, C), bf16), hb=V((16, L), bf16), xp=V((4, L + 8, L), f32), bp=V((L + 8, L), f32),
        bslope=V((L, L), f32), bcv=V((L, L), f32), b2=V((L, L), bf16), c2=V((L, L), bf16),
        bt3=V((128, 768), bf16), ct3=V((128, 768), bf16), x=V((4, L, L), f32),
        slope=V((4, L, L), f32), xend=V((4, 2 * L, L), bf16), pst=V((8, 136, 128), f32),
        poth=V((8, 136, 128), f32), sc=V((L, L), f32), sct=V((L, L), f32), diag=V((L, 128), f32),
        sm=V((DENSE, L, 2 * L), bf16), smt=V((DENSE, L, 2 * L), bf16),
        wm=V((WIDE, 128, L), bf16), wmt=V((WIDE, 128, L), bf16), wx=V((WIDE, 4, L, L), bf16),
        wds=V((128, 128), f32), bgw=V((L, 128), f32), wg=V((WIDE, 4, L, L), bf16),
        ef=V((DENSE, 4, L, L), f32), we=V((WIDE, 4, 128, L), f32),
        wa=V((WIDE, 4, 128, L), f32), ga2=V((DENSE, 4, 2 * L, L), bf16), acc=V((4, L, L), f32),
        xe=V((DENSE, 4, 2 * L, L), bf16), ps=V((4, 136, 128), f32), xr=V((4, 136, 128), f32),
        ff=V((nf - 1, 2, 4, 128, 128), f32), cf=V((8, 8, 128), f32), df=V((8, 8, 128), f32),
        zs=V((nz, 136, 128), f32), zr=V((nz, 136, 128), f32), fb=V((2, 128, 128), f32),
        bx=V((4, 8, 128), f32), befs=V((nz, 8, 128), f32), fst=V((nz, 4, 128, 128), f32),
        fhl=V((nf, 4, L, L), bf16), st=V((2, L, 128), f32), gact=V((4, L, L), f32),
        g=V((4, L, L), f32), sts=V((8, L), f32), str=V((max(Y - 1, 1), 8, L), f32),
        inv=V((L, 128), f32), kk=V((L, 128), f32), gf=V((nf, 8, 128, 128), f32),
        go=V((nf - 1, 4, 128, 128), f32), ga=V((nf - 1, 4, 128, 128), f32),
        gx=V((nf - 1, 4, 128, 128), f32), g0r=V((8, 128, 128), f32), ds=V((L, L), f32),
        dsk=V((L, L), f32), cg=V((L, 128), f32), dv=V((L, 128), f32), dx=V((4, L, L), f32),
        dzs=V((nz, 128, 128), f32), dzr=V((nz, 128, 128), f32), dcur=V((128, 128), f32),
        dps=V((4, 128, 128), f32), dph=V((8, 128, 128), f32), bce=V((ny + 1, L, L), f32),
        bcer=V((max(ny, 1), L, L), f32), bl=V((ny + 1, L, 128), f32),
        blr=V((max(ny, 1), L, 128), f32), bs=V((ny + 1, 8, 128), f32), bsr=V((max(ny, 1), 8, 128), f32),
        nbs=V((8, L), f32), nbe=V((8, L), f32), hxs=V((8, C), f32), hxr=V((8, C), f32),
        ssem=pltpu.SemaphoreType.DMA((96,)), rsem=pltpu.SemaphoreType.DMA((96,)),
    )

    def per_device(x_raw, bc_raw, gate_raw, log_decay, level_weights, conv_x, conv_bc, gain, og):
        spec = pl.BlockSpec(memory_space=pltpu.VMEM)
        return pl.pallas_call(
            functools.partial(kernel, Z, Y, list(shapes)),
            out_shape=(
                jax.ShapeDtypeStruct((L, C), bf16),
                jax.ShapeDtypeStruct((L, C), bf16),
                jax.ShapeDtypeStruct((L, L), bf16),
            ),
            in_specs=[spec] * 9,
            out_specs=(spec,) * 3,
            scratch_shapes=list(shapes.values()),
            compiler_params=pltpu.CompilerParams(
                collective_id=0, has_side_effects=True, vmem_limit_bytes=67043328
            ),
        )(
            x_raw, bc_raw, gate_raw, og, log_decay, level_weights, conv_x, conv_bc,
            gain.reshape(1, C),
        )

    in_specs = (
        P("ctx", "head"), P("ctx", None), P("ctx", "head"), P("head", "ctx"),
        P(None, "head", "ctx"), P(None, "head"), P(), P("head"), P("ctx", "head"),
    )
    out_specs = (P("ctx", "head"), P("ctx", "head"), P("ctx", None))
    return jax.shard_map(
        per_device, mesh=mesh, in_specs=in_specs, out_specs=out_specs, check_vma=False
    )
```

```python
import functools

import jax
import jax.numpy as jnp
from jax import lax
from jax.experimental import pallas as pl
from jax.experimental.pallas import tpu as pltpu
from jax.sharding import PartitionSpec as P

MESH = pl.DeviceIdType.MESH
f32 = jnp.float32
bf16 = jnp.bfloat16
L = 256
C = 1024
INNER = 4096
EPS = 1e-05
LEV = 8
DENSE = 4
WIDE = LEV - DENSE


def split(v):
    hi = v.astype(bf16)
    return hi, (v - hi.astype(f32)).astype(bf16)


def mm(a, b):
    return jnp.dot(a, b, preferred_element_type=f32)


def mt(a, b):
    return lax.dot_general(a, b, (((1,), (1,)), ((), ())), preferred_element_type=f32)


def cat(parts, axis):
    return jnp.concatenate(parts, axis=axis)


def mm3(ah, al, bh, bl):
    return mm(cat([ah, ah, al], 1), cat([bh, bl, bh], 0))


def mt3(ah, al, bh, bl):
    return mt(cat([ah, ah, al], 1), cat([bh, bl, bh], 1))


def loop(n, fn, unroll=1):
    def step(i, carry):
        for t in range(unroll):
            fn(i * unroll + t)
        return carry

    lax.fori_loop(0, n // unroll, step, 0)


def sigmoid(v):
    return 1.0 / (1.0 + jnp.exp(-v))


def kernel(
    Z, Y, names,
    x_ref, bc_ref, gate_ref, og_ref, ld_ref, lw_ref, tx_ref, tb_ref, gain_ref,
    out_ref, xg_ref, bg_ref, *scratch,
):
    r = dict(zip(names, scratch))
    nz = Z.bit_length() - 1
    nctx = Z * 8
    nf = 3 + nz
    ctx = lax.axis_index("ctx")
    hd = lax.axis_index("head")
    core = ctx % 2
    xx = (ctx // 2) % 4
    zz = ctx // 8
    core_f = core.astype(f32)
    ssem, rsem = r["ssem"], r["rsem"]
    ids = {}

    def rc(key, src, dst, dev):
        i = ids.setdefault(key, len(ids))
        return pltpu.make_async_remote_copy(
            src_ref=src, dst_ref=dst, send_sem=ssem.at[i], recv_sem=rsem.at[i],
            device_id=dev, device_id_type=MESH,
        )

    def at_x(q):
        return (zz * 8 + q * 2 + core, hd)

    def mirror(m):
        w = 2 ** (m + 1)
        return ((zz // w) * w + (w - 1) - zz % w) * 8 + xx * 2 + core

    def zbit(m):
        return (zz // 2**m) % 2

    other = (ctx + 1 - 2 * core, hd)
    following = ((ctx + 1) % nctx, hd)
    preceding = ((ctx + nctx - 1) % nctx, hd)

    def cbit(l):
        if l == 1:
            return xx % 2
        if l == 2:
            return xx // 2
        return zbit(l - 3)

    peers = [other, following, preceding]
    peers += [at_x((xx + d) % 4) for d in (1, 2, 3)]
    peers += [(mirror(m), hd) for m in range(nz)]
    peers += [(ctx, (hd + d) % Y) for d in range(1, Y)]
    yp = []
    w = 2
    while w <= Y:
        yp.append((ctx, (hd // w) * w + (w - 1) - hd % w))
        w *= 2
    barrier = pltpu.get_barrier_semaphore()
    for dev in peers:
        pl.semaphore_signal(barrier, inc=1, device_id=dev, device_id_type=MESH)

    pend = []

    def cols(j):
        return pl.ds(pl.multiple_of(j * 256, 256), 256)

    row = lax.broadcasted_iota(jnp.int32, (L, L), 0)
    col = lax.broadcasted_iota(jnp.int32, (L, L), 1)
    dist = row ^ col
    r["zle"][...] = jnp.where(row <= col, dist, 4096)
    r["zgt"][...] = jnp.where(row > col, dist, 4096)
    r["zlt"][...] = jnp.where(row < col, dist, 4096)

    def make_ex(o):
        a = lax.broadcasted_iota(jnp.int32, (L, L), 0) % 128
        b = lax.broadcasted_iota(jnp.int32, (L, L), 1) // 64
        r["ex"][o] = jnp.where(a == b + 4 * o, 1.0, 0.0).astype(bf16)

    loop(32, make_ex)
    pl.semaphore_wait(barrier, len(peers))
    hx = rc("hx", x_ref.at[L - 16 : L], r["hx"], following)
    hb = rc("hb", bc_ref.at[L - 16 : L], r["hb"], following)
    hx.start()
    hb.start()
    pend += [hx, hb]
    ld = ld_ref[...]
    l0 = ld.astype(bf16)
    rest = ld - l0.astype(f32)
    l1 = rest.astype(bf16)
    l2 = (rest - l1.astype(f32)).astype(bf16)
    r["ld"][...] = cat([l0, l1, l2], 0)
    q = r["q"]

    def sums(mask):
        t = mm(r["ld"][...], jnp.where(mask, 1.0, 0.0).astype(bf16))
        return t[0:16] + t[16:32] + t[32:48]

    def coefs(k):
        th = lax.shift_left(jnp.int32(1), k)
        up = sums(r["zle"][...] < th)
        dn = sums(r["zgt"][...] < th)
        at = pl.ds(pl.multiple_of(k * 16, 16), 16)
        q[0, at, :] = lw_ref[k + 1] * jnp.exp(up)
        q[1, at, :] = jnp.exp(dn)

    loop(LEV, coefs)
    up = sums(r["zle"][...] < L)
    dn = sums(r["zgt"][...] < L)
    eup = jnp.exp(up)
    for l in range(nf):
        q[2, l * 16 : l * 16 + 16, :] = lw_ref[min(LEV + 1 + l, 15)] * eup
    for l in range(nf, 6):
        q[2, l * 16 : l * 16 + 16, :] = jnp.zeros((16, L), f32)
    q[2, 96:112, :] = jnp.exp(dn)
    q[2, 112:128, :] = jnp.broadcast_to(eup[:, L - 1 : L], (16, L))
    q[3] = jnp.zeros((128, L), f32)
    q[3, 0:16, :] = lw_ref[0]
    for g in range(4):
        hi, lo = split(q[g].T)
        r["qt"][g, :, 0:128] = hi
        r["qt"][g, :, 128:256] = lo

    def spread(g, i, j):
        return mm(r["qt"][g], r["ex"][i * 4 + j])

    xp, bp = r["xp"], r["bp"]

    def widen(j):
        xp[j, 8 : L + 8, :] = x_ref[:, cols(j)].astype(f32)

    loop(4, widen)
    bp[8 : L + 8, :] = bc_ref[...].astype(f32)
    has_prev = jnp.where(ctx > 0, 1.0, 0.0).astype(f32)
    hx.wait_recv()
    hb.wait_recv()
    for j in range(4):
        xp[j, 0:8, :] = r["hx"][:, j * 256 : j * 256 + 256].astype(f32)[8:16] * has_prev
    bp[0:8, :] = r["hb"][...].astype(f32)[8:16] * has_prev

    bpre = tb_ref[0:1] * bp[5 : L + 5, :]
    for k in range(1, 4):
        bpre = bpre + tb_ref[k : k + 1] * bp[5 + k : L + 5 + k, :]
    bsig = sigmoid(bpre)
    r["bslope"][...] = bsig * (1.0 + bpre * (1.0 - bsig))
    nbs = rc("nbs", r["bslope"].at[0:8], r["nbs"], preceding)
    nbs.start()
    pend.append(nbs)
    bcv = bpre * bsig
    r["bcv"][...] = bcv
    b = bcv[:, 0:128]
    c = bcv[:, 128:256]
    bh, bl = split(b)
    ch, cl = split(c)
    bth, btl = split(b.T)
    cth, ctl = split(c.T)
    r["b2"][...] = cat([bh, bl], 1)
    r["c2"][...] = cat([ch, cl], 1)
    r["bt3"][...] = cat([bth, bth, btl], 1)
    r["ct3"][...] = cat([cth, cth, ctl], 1)
    pst = r["pst"]

    def conv(j):
        pre = tx_ref[0:1, cols(j)] * xp[j, 5 : L + 5, :]
        for k in range(1, 4):
            pre = pre + tx_ref[k : k + 1, cols(j)] * xp[j, 5 + k : L + 5 + k, :]
        sig = sigmoid(pre)
        x = pre * sig
        r["x"][j] = x
        r["slope"][j] = sig * (1.0 + pre * (1.0 - sig))
        hi, lo = split(x * spread(2, 6, j))
        r["xend"][j, 0:L] = hi
        r["xend"][j, L : 2 * L] = lo
        s = mm(r["bt3"][...], cat([hi, lo, hi], 0))
        d = mm(r["qt"][2, 0:16, :], r["ex"][28 + j])[0:8]
        for h in range(2):
            pst[2 * j + h, 0:128] = s[:, h * 128 : h * 128 + 128]
            pst[2 * j + h, 128:136] = d[:, h * 128 : h * 128 + 128]

    loop(4, conv)

    p0 = rc("p0", pst, r["poth"], other)
    p0.start()
    pend.append(p0)
    poth = r["poth"]

    sc = mt3(ch, cl, bh, bl)
    sct = mt3(bh, bl, ch, cl)
    r["sc"][...] = sc
    r["sct"][...] = sct
    diag = jnp.sum(c * b, axis=1, keepdims=True)
    r["diag"][...] = jnp.broadcast_to(diag, (L, 128))

    def level_masks(k):
        th = lax.shift_left(jnp.int32(1), k)
        z = r["zgt"][...]
        hi, lo = split(jnp.where((z >= th) & (z < 2 * th), r["sc"][...], 0.0))
        r["sm"][k, :, 0:L] = hi
        r["sm"][k, :, L : 2 * L] = lo
        z = r["zlt"][...]
        hi, lo = split(jnp.where((z >= th) & (z < 2 * th), r["sct"][...], 0.0))
        r["smt"][k, :, 0:L] = hi
        r["smt"][k, :, L : 2 * L] = lo

    loop(DENSE, level_masks)

    def low(k, get):
        h = 2**k
        return cat([get(s, s + h) for s in range(0, L, 2 * h)], 0)

    def upp(k, get):
        h = 2**k
        return cat([get(s + h, s + 2 * h) for s in range(0, L, 2 * h)], 0)

    def same(k):
        u = lax.broadcasted_iota(jnp.int32, (128, 128), 0) // 2**k
        v = lax.broadcasted_iota(jnp.int32, (128, 128), 1) // 2**k
        return u == v

    for k in range(DENSE, LEV):
        cu = upp(k, lambda a, b: r["c2"][a:b])
        bw = low(k, lambda a, b: r["b2"][a:b])
        cuh, cul, bwh, bwl = cu[:, 0:128], cu[:, 128:256], bw[:, 0:128], bw[:, 128:256]
        w = k - DENSE
        hi, lo = split(jnp.where(same(k), mt3(cuh, cul, bwh, bwl), 0.0))
        r["wm"][w, :, 0:128] = hi
        r["wm"][w, :, 128:256] = lo
        hi, lo = split(jnp.where(same(k), mt3(bwh, bwl, cuh, cul), 0.0))
        r["wmt"][w, :, 0:128] = hi
        r["wmt"][w, :, 128:256] = lo

    def near(j):
        dg = r["diag"][...]
        r["acc"][j] = spread(3, 0, j) * (cat([dg, dg], 1) * r["x"][j])

        def level(k):
            e = spread(1, k, j)
            r["ef"][k, j] = e
            hi, lo = split(r["x"][j] * e)
            r["xe"][k, j, 0:L] = hi
            r["xe"][k, j, L : 2 * L] = lo
            m = r["sm"][k]
            y = mm(cat([m[:, 0:L], m], 1), cat([hi, lo, hi], 0))
            a = spread(0, k, j)
            r["acc"][j] = r["acc"][j] + a * y

        loop(DENSE, level, 2)
        for k in range(DENSE, LEV):
            w, h = k - DENSE, 2**k
            e = mm(low(k, lambda a, b: r["qt"][1, a:b]), r["ex"][k * 4 + j])
            r["we"][w, j] = e
            hi, lo = split(low(k, lambda a, b: r["x"][j, a:b]) * e)
            r["wx"][w, j, 0:128] = hi
            r["wx"][w, j, 128:256] = lo
            m = r["wm"][w]
            y = mm(cat([m[:, 0:128], m], 1), cat([hi, lo, hi], 0))
            a = mm(upp(k, lambda a, b: r["qt"][0, a:b]), r["ex"][k * 4 + j])
            r["wa"][w, j] = a
            y = y * a
            for i in range(128 // h):
                at = slice((2 * i + 1) * h, (2 * i + 2) * h)
                r["acc"][j, at] = r["acc"][j, at] + y[i * h : (i + 1) * h]

    p0.wait_recv()
    ps, xr, ff = r["ps"], r["xr"], r["ff"]
    for h in range(4):
        own = pst[core * 4 + h]
        oth = poth[core * 4 + h]
        lo = jnp.where(core == 0, own, oth)
        hi = jnp.where(core == 0, oth, own)
        ps[h, 0:128] = lo[0:128] * hi[128:129] + hi[0:128]
        ps[h, 128:136] = lo[128:136] * hi[128:136]
    xr[xx] = ps[xx]
    for p in range(8):
        dd = poth[p, 128:136]
        r["cf"][p] = jnp.where(core == 1, dd, 1.0)
        r["df"][p] = jnp.where(core == 0, dd, 1.0)
    xs = []
    for d in (1, 2, 3):
        to = (xx + d) % 4
        xs.append(rc(("xs", d), ps.at[to], xr.at[xx], at_x(to)))
        xs[-1].start()
    pend += xs

    near(0)
    near(1)

    for cp in xs:
        cp.wait_recv()
    dec = [xr[i, 128:129] for i in range(4)]
    b01 = xr[0, 0:128] * dec[1] + xr[1, 0:128]
    b23 = xr[2, 0:128] * dec[3] + xr[3, 0:128]
    d01 = dec[0] * dec[1]
    d23 = dec[2] * dec[3]
    zs, zr, fb, bx, befs = r["zs"], r["zr"], r["fb"], r["bx"], r["befs"]
    zs[0, 0:128] = b01 * d23 + b23
    zs[0, 128:136] = jnp.broadcast_to(d01 * d23, (8, 128))
    fb[0] = b01
    fb[1] = b01 * dec[2]
    bx[0] = jnp.ones((8, 128), f32)
    bx[1] = jnp.broadcast_to(dec[0], (8, 128))
    bx[2] = jnp.broadcast_to(d01, (8, 128))
    bx[3] = jnp.broadcast_to(d01 * dec[2], (8, 128))
    befs[0] = jnp.ones((8, 128), f32)

    def z_copy(m):
        return rc(("z", m), zs.at[m], zr.at[m], (mirror(m), hd))

    def z_start(m):
        if m < nz - 1:
            z_copy(m).start()
        else:
            @pl.when(zbit(m) == 0)
            def _():
                z_copy(m).start()

    def f_copy(l, d):
        to = (xx + d) % 4
        if l == 1:
            src = xr.at[(to + 3) % 4, 0:128]
        elif l == 2:
            src = fb.at[to % 2]
        else:
            src = r["fst"].at[l - 3, to]
        return rc(("f", l, d), src, ff.at[l - 1, core, xx], at_x(to))

    def to_bit(l, d):
        to = (xx + d) % 4
        return to % 2 if l == 1 else to // 2 if l == 2 else zbit(l - 3)

    def from_bit(l, d):
        fr = (xx + 4 - d) % 4
        return fr % 2 if l == 1 else fr // 2 if l == 2 else zbit(l - 3)

    def f_send(l):
        for d in (1, 2, 3):
            @pl.when(to_bit(l, d) == 1)
            def _():
                f_copy(l, d).start()

    def fo_copy(l):
        return rc(("fo", l), ff.at[l - 1, core], ff.at[l - 1, core], other)

    def f_relay(l):
        @pl.when(cbit(l) == 1)
        def _():
            for d in (1, 2, 3):
                f_copy(l, d).wait_recv()
            fo_copy(l).start()

    z_start(0)

    @pl.when(xx % 2 == 1)
    def _():
        ff[0, core, xx] = xr[(xx + 3) % 4, 0:128]

    @pl.when(xx // 2 == 1)
    def _():
        ff[1, core, xx] = fb[xx % 2]

    f_send(2)
    f_send(1)

    def z_done(m):
        up = zbit(m)

        @pl.when(up == 1)
        def _():
            z_copy(m).wait_recv()
            f = zr[m, 0:128] * befs[m, 0:1]
            for i in range(4):
                r["fst"][m, i] = f * bx[i, 0:1]
            ff[2 + m, core, xx] = f * bx[xx, 0:1]
            if m < nz - 1:
                zs[m + 1, 0:128] = zr[m, 0:128] * zs[m, 128:129] + zs[m, 0:128]
                befs[m + 1] = befs[m] * zr[m, 128:136]

        if m < nz - 1:
            @pl.when(up == 0)
            def _():
                z_copy(m).wait_recv()
                zs[m + 1, 0:128] = zs[m, 0:128] * zr[m, 128:129] + zr[m, 0:128]
                befs[m + 1] = befs[m]

            zs[m + 1, 128:136] = zs[m, 128:136] * zr[m, 128:136]
            z_start(m + 1)
        f_send(3 + m)

    near(2)
    z_done(0)
    near(3)
    f_relay(2)
    f_relay(1)

    fhl = r["fhl"]

    def inter(l, j, f):
        hi, lo = split(f)
        fhl[l, j, 0:128] = hi
        fhl[l, j, 128:256] = lo
        c2 = r["c2"][...]
        y = mm(cat([c2[:, 0:128], c2[:, 0:128]], 1), cat([hi, lo], 0)) + mm(c2[:, 128:256], hi)
        r["acc"][j] = r["acc"][j] + spread(2, l, j) * y

    @pl.when(core == 1)
    def _():
        def f0(j):
            inter(0, j, cat([poth[2 * j, 0:128], poth[2 * j + 1, 0:128]], 1))

        loop(4, f0)

    def far(l):
        @pl.when(cbit(l) == 1)
        def _():
            fo_copy(l).wait_recv()

            def one(j):
                parts = [
                    ff[l - 1, j // 2, (j % 2) * 2 + h] * r["cf"][2 * j + h, 0:1] for h in range(2)
                ]
                inter(l, j, cat(parts, 1))

            loop(4, one, 2)

    if nz > 1:
        z_done(1)
    f_relay(3)
    far(2)
    far(1)

    def gate_first(j):
        g = gate_ref[:, cols(j)].astype(f32)
        r["gact"][j] = g * sigmoid(g)
        r["g"][j] = gain_ref[:, cols(j)] * og_ref[:, cols(j)].astype(f32)

    loop(4, gate_first)
    for m in range(2, nz):
        z_done(m)
        if m == 2:
            f_relay(4)
    far(3)
    for l in range(4, nf):
        if l > 4 or nz <= 2:
            f_relay(l)
        far(l)

    r["st"][...] = jnp.zeros((2, L, 128), f32)

    def gated(j):
        mixed = r["acc"][j] * r["gact"][j]
        r["acc"][j] = mixed
        sg = r["g"][j]
        sq = mixed * mixed
        cr = sg * mixed
        r["st"][0] = r["st"][0] + (sq[:, 0:128] + sq[:, 128:256])
        r["st"][1] = r["st"][1] + (cr[:, 0:128] + cr[:, 128:256])

    loop(4, gated)
    s0 = jnp.sum(r["st"][0], axis=1, keepdims=True)
    s1 = jnp.sum(r["st"][1], axis=1, keepdims=True)
    lane = lax.broadcasted_iota(jnp.int32, (L, 128), 1)
    both = jnp.where(lane == 0, s0, s1)
    r["sts"][...] = both.T[0:8]
    ys = []
    for d in range(1, Y):
        ys.append(rc(("st", d), r["sts"], r["str"].at[d - 1], (ctx, (hd + d) % Y)))
        ys[-1].start()
    pend += ys
    tot = r["sts"][...]
    for d in range(1, Y):
        ys[d - 1].wait_recv()
        tot = tot + r["str"][d - 1]
    inv_row = lax.rsqrt(tot[0:1] / INNER + EPS)
    k_row = inv_row * inv_row * inv_row * (tot[1:2] / INNER)
    r["inv"][...] = jnp.broadcast_to(inv_row, (128, L)).T
    r["kk"][...] = jnp.broadcast_to(k_row, (128, L)).T

    def normed(j):
        inv = cat([r["inv"][...]] * 2, 1)
        kk = cat([r["kk"][...]] * 2, 1)
        mixed = r["acc"][j]
        out_ref[:, cols(j)] = (gain_ref[:, cols(j)] * mixed * inv).astype(bf16)
        r["g"][j] = (r["g"][j] * inv - mixed * kk) * r["gact"][j]

    loop(4, normed)

    gf, go, ga_, gx = r["gf"], r["go"], r["ga"], r["gx"]

    def go_copy(l):
        return rc(("go", l), gf.at[l, pl.ds((1 - core) * 4, 4)], go.at[l - 1], other)

    def far_grad(l):
        def one(j):
            hi, lo = split(r["g"][j] * spread(2, l, j))
            s = mm(r["ct3"][...], cat([hi, lo, hi], 0))
            r["cg"][...] = r["cg"][...] + mt3(hi, lo, fhl[l, j, 0:128], fhl[l, j, 128:256])
            for h in range(2):
                piece = s[:, h * 128 : h * 128 + 128]
                if l > 0:
                    piece = piece * r["cf"][2 * j + h, 0:1]
                gf[l, 2 * j + h] = piece

        loop(4, one, 2)

    def g0_copy():
        return rc("g0", gf.at[0], r["g0r"], other)

    def gx_copy(l, d):
        to = (xx + d) % 4
        return rc(("gx", l, d), ga_.at[l - 1, to], gx.at[l - 1, xx], at_x(to))

    def g_pair(l):
        @pl.when(cbit(l) == 1)
        def _():
            go_copy(l).wait_recv()
            for h in range(4):
                ga_[l - 1, h] = gf[l, core * 4 + h] + go[l - 1, h]
            for d in (1, 2, 3):
                gx_copy(l, d).start()
            gx[l - 1, xx] = ga_[l - 1, xx]

    def fg(l):
        @pl.when((core if l == 0 else cbit(l)) == 1)
        def _():
            far_grad(l)
            (go_copy(l) if l else g0_copy()).start()

    r["ds"][...] = jnp.zeros((L, L), f32)
    r["cg"][...] = jnp.zeros((L, 128), f32)
    r["bgw"][...] = jnp.zeros((L, 128), f32)

    fg(nf - 1)
    for l in range(nf - 2, -1, -1):
        fg(l)
        g_pair(l + 1)

    def first_dx(j):
        dg = r["diag"][...]
        gw = r["g"][j] * spread(3, 0, j)
        r["dx"][j] = gw * cat([dg, dg], 1)
        pr = gw * r["x"][j]
        r["dv"][...] = r["dv"][...] + (pr[:, 0:128] + pr[:, 128:256])

    r["dv"][...] = jnp.zeros((L, 128), f32)
    loop(4, first_dx)

    def near_ds(k):
        r["dsk"][...] = jnp.zeros((L, L), f32)

        def one(j):
            hi, lo = split(r["g"][j] * spread(0, k, j))
            r["ga2"][k, j, 0:L] = hi
            r["ga2"][k, j, L : 2 * L] = lo
            eh = r["xe"][k, j, 0:L]
            el = r["xe"][k, j, L : 2 * L]
            r["dsk"][...] = r["dsk"][...] + mt3(hi, lo, eh, el)

        loop(4, one, 2)
        th = lax.shift_left(jnp.int32(1), k)
        z = r["zgt"][...]
        r["ds"][...] = r["ds"][...] + jnp.where((z >= th) & (z < 2 * th), r["dsk"][...], 0.0)

    def near_dx(k):
        def one(j):
            hi = r["ga2"][k, j, 0:L]
            lo = r["ga2"][k, j, L : 2 * L]
            m = r["smt"][k]
            y = mm(cat([m[:, 0:L], m], 1), cat([hi, lo, hi], 0))
            r["dx"][j] = r["dx"][j] + r["ef"][k, j] * y

        loop(4, one, 2)

    def wide_ds(k):
        w, h = k - DENSE, 2**k
        r["wds"][...] = jnp.zeros((128, 128), f32)

        def one(j):
            hi, lo = split(upp(k, lambda a, b: r["g"][j, a:b]) * r["wa"][w, j])
            r["wg"][w, j, 0:128] = hi
            r["wg"][w, j, 128:256] = lo
            eh = r["wx"][w, j, 0:128]
            el = r["wx"][w, j, 128:256]
            r["wds"][...] = r["wds"][...] + mt3(hi, lo, eh, el)

        loop(4, one, 2)
        d = jnp.where(same(k), r["wds"][...], 0.0)
        dh, dl = split(d)
        th, tl = split(d.T)
        cu = upp(k, lambda a, b: r["c2"][a:b])
        bw = low(k, lambda a, b: r["b2"][a:b])
        cg = mm3(dh, dl, bw[:, 0:128], bw[:, 128:256])
        bg = mm3(th, tl, cu[:, 0:128], cu[:, 128:256])
        for i in range(128 // h):
            at = slice(2 * i * h, (2 * i + 1) * h)
            r["bgw"][at] = r["bgw"][at] + bg[i * h : (i + 1) * h]
            at = slice((2 * i + 1) * h, (2 * i + 2) * h)
            r["cg"][at] = r["cg"][at] + cg[i * h : (i + 1) * h]

    def wide_dx(k):
        w, h = k - DENSE, 2**k

        def one(j):
            hi = r["wg"][w, j, 0:128]
            lo = r["wg"][w, j, 128:256]
            m = r["wmt"][w]
            y = mm(cat([m[:, 0:128], m], 1), cat([hi, lo, hi], 0)) * r["we"][w, j]
            for i in range(128 // h):
                at = slice(2 * i * h, (2 * i + 1) * h)
                r["dx"][j, at] = r["dx"][j, at] + y[i * h : (i + 1) * h]

        loop(4, one, 2)

    def dense(fn, lo, hi):
        def step(k, carry):
            fn(k)
            return carry

        lax.fori_loop(lo, hi, step, 0)

    dzs, dzr, dcur = r["dzs"], r["dzr"], r["dcur"]

    def dz_copy(m):
        return rc(("dz", m), dzs.at[m], dzr.at[m], (mirror(m), hd))

    def dz_start(m):
        last = m == nz - 1

        @pl.when(zbit(m) == 1)
        def _():
            for d in (1, 2, 3):
                gx_copy(3 + m, d).wait_recv()
            f = gx[2 + m, 0]
            for i in range(1, 4):
                f = f + gx[2 + m, i] * bx[i, 0:1]
            f = f * befs[m, 0:1]
            if not last:
                f = f + dcur[...] * zs[m, 128:129]
            dzs[m] = f
            dz_copy(m).start()

        if not last:
            @pl.when(zbit(m) == 0)
            def _():
                dzs[m] = dcur[...]
                dz_copy(m).start()

    def dz_done(m):
        if m == nz - 1:
            @pl.when(zbit(m) == 1)
            def _():
                dcur[...] = jnp.zeros((128, 128), f32)

            @pl.when(zbit(m) == 0)
            def _():
                dz_copy(m).wait_recv()
                dcur[...] = dzr[m]
        else:
            dz_copy(m).wait_recv()

            @pl.when(zbit(m) == 1)
            def _():
                dcur[...] = dcur[...] + dzr[m]

            @pl.when(zbit(m) == 0)
            def _():
                dcur[...] = dcur[...] * zr[m, 128:129] + dzr[m]

    dz_start(nz - 1)
    dense(near_ds, 0, DENSE)
    if nz > 1:
        dz_done(nz - 1)
        dz_start(nz - 2)
    for k in range(DENSE, LEV):
        wide_ds(k)
    if nz == 1:
        dz_done(0)
    ds = r["ds"][...]
    dsh, dsl = split(ds)
    dth, dtl = split(ds.T)
    b2 = r["b2"][...]
    c2 = r["c2"][...]
    dv = jnp.sum(r["dv"][...], axis=1, keepdims=True)
    cg = r["cg"][...] + mm3(dsh, dsl, b2[:, 0:128], b2[:, 128:256]) + dv * r["bcv"][:, 0:128]
    bg = r["bgw"][...] + mm3(dth, dtl, c2[:, 0:128], c2[:, 128:256]) + dv * r["bcv"][:, 128:256]
    r["bce"][0, :, 0:128] = bg
    r["bce"][0, :, 128:256] = cg
    def y_start(key, src, dst, step):
        cp = rc((key, step), src.at[step], dst.at[step], yp[step])
        cp.start()
        pend.append(cp)
        return cp

    def y_sum(key, src, dst, step):
        rc((key, step), src.at[step], dst.at[step], yp[step]).wait_recv()
        src[step + 1] = src[step] + dst[step]

    ny = len(yp)
    if ny:
        y_start("be", r["bce"], r["bcer"], 0)

    for m in range(nz - 2, -1, -1):
        dz_done(m)
        if m:
            dz_start(m - 1)
        if m == nz - 2:
            dense(near_dx, 0, 2)

    dps, dph = r["dps"], r["dph"]
    for l in (1, 2):
        for d in (1, 2, 3):
            @pl.when(from_bit(l, d) == 1)
            def _():
                gx_copy(l, d).wait_recv()

    dt = dcur[...]
    dec = [xr[i, 128:129] for i in range(4)]
    d01 = dt * (dec[2] * dec[3]) + (gx[1, 2] + gx[1, 3] * dec[2])
    dps[0] = d01 * dec[1] + gx[0, 1]
    dps[1] = d01
    dps[2] = dt * dec[3] + gx[0, 3]
    dps[3] = dt
    dpc = []
    for d in (1, 2, 3):
        to = (xx + d) % 4
        dpc.append(rc(("dp", d), dps.at[to], dph.at[core * 4 + xx], at_x(to)))
        dpc[-1].start()
    pend += dpc
    dph[core * 4 + xx] = dps[xx]

    dense(near_dx, 2 if nz > 1 else 0, DENSE)
    wide_dx(DENSE)
    if ny > 1:
        y_sum("be", r["bce"], r["bcer"], 0)
        y_start("be", r["bce"], r["bcer"], 1)
    for k in range(DENSE + 1, LEV):
        wide_dx(k)

    for cp in dpc:
        cp.wait_recv()
    half = pl.ds(core * 4, 4)
    dpo = rc("dpo", dph.at[half], dph.at[half], other)
    dpo.start()

    dpo.wait()

    @pl.when(core == 0)
    def _():
        g0_copy().wait_recv()
        for p in range(8):
            dph[p] = dph[p] * r["df"][p, 0:1] + r["g0r"][p]

    r["bl"][0] = jnp.zeros((L, 128), f32)
    xsl = r["xp"]

    def last_dx(j):
        hi, lo = split(cat([dph[2 * j], dph[2 * j + 1]], 1))
        r["bl"][0] = r["bl"][0] + mt3(r["xend"][j, 0:L], r["xend"][j, L : 2 * L], hi, lo)
        b2 = r["b2"][...]
        y = mm(cat([b2[:, 0:128], b2[:, 0:128]], 1), cat([hi, lo], 0)) + mm(b2[:, 128:256], hi)
        dx = r["dx"][j] + spread(2, 6, j) * y
        sl = dx * r["slope"][j]
        xsl[j, 0:L] = sl
        r["hxs"][:, cols(j)] = sl[0:8]

    loop(4, last_dx)
    nx = rc("nx", r["hxs"], r["hxr"], preceding)
    nx.start()
    n8 = rc("n8", r["bl"].at[0, 0:8], r["bs"].at[0], preceding)
    n8.start()
    pend += [nx, n8]
    if ny:
        y_start("bl", r["bl"], r["blr"], 0)
    for i in range(min(1, ny - 1), ny):
        y_sum("be", r["bce"], r["bcer"], i)
        if i < ny - 1:
            y_start("be", r["bce"], r["bcer"], i + 1)
    n8.wait_recv()
    if ny:
        y_start("bs", r["bs"], r["bsr"], 0)
    nbe = rc("nbe", r["bce"].at[ny, 0:8], r["nbe"], preceding)
    nbe.start()
    pend.append(nbe)
    has_next = jnp.where(ctx < nctx - 1, 1.0, 0.0).astype(f32)

    nx.wait_recv()
    for j in range(4):
        xsl[j, L : L + 8] = r["hxr"][:, j * 256 : j * 256 + 256] * has_next

    def conv_back(j):
        v = tx_ref[3:4, cols(j)] * xsl[j, 0:L]
        for k in range(3):
            v = v + tx_ref[k : k + 1, cols(j)] * xsl[j, 3 - k : L + 3 - k]
        xg_ref[:, cols(j)] = v.astype(bf16)

    loop(4, conv_back)
    for i in range(ny):
        y_sum("bl", r["bl"], r["blr"], i)
        y_sum("bs", r["bs"], r["bsr"], i)
        if i < ny - 1:
            y_start("bl", r["bl"], r["blr"], i + 1)
            y_start("bs", r["bs"], r["bsr"], i + 1)
    total = r["bce"][ny]
    bp[0:L, :] = cat([total[:, 0:128] + r["bl"][ny], total[:, 128:256]], 1) * r["bslope"][...]
    nbs.wait_recv()
    nbe.wait_recv()
    total = r["nbe"][...]
    rows = cat([total[:, 0:128] + r["bs"][ny], total[:, 128:256]], 1)
    bp[L : L + 8, :] = rows * r["nbs"][...] * has_next
    v = tb_ref[3:4] * bp[0:L, :]
    for k in range(3):
        v = v + tb_ref[k : k + 1] * bp[3 - k : L + 3 - k, :]
    bg_ref[...] = v.astype(bf16)

    for cp in pend:
        cp.wait_send()
    for m in range(nz):
        if m < nz - 1:
            z_copy(m).wait_send()
            dz_copy(m).wait_send()
        else:
            @pl.when(zbit(m) == 0)
            def _():
                z_copy(m).wait_send()

            @pl.when(zbit(m) == 1)
            def _():
                dz_copy(m).wait_send()
    for l in range(1, nf):
        for d in (1, 2, 3):
            @pl.when(to_bit(l, d) == 1)
            def _():
                f_copy(l, d).wait_send()

        @pl.when(cbit(l) == 1)
        def _():
            fo_copy(l).wait_send()
            go_copy(l).wait_send()
            for d in (1, 2, 3):
                gx_copy(l, d).wait_send()

    @pl.when(core == 1)
    def _():
        g0_copy().wait_send()


def solution(mesh):
    nctx, Y = mesh.shape["ctx"], mesh.shape["head"]
    Z = nctx // 8
    nz = Z.bit_length() - 1
    nf = 3 + nz
    ny = Y.bit_length() - 1
    V = pltpu.VMEM
    shapes = dict(
        zle=V((L, L), jnp.int32), zgt=V((L, L), jnp.int32), zlt=V((L, L), jnp.int32),
        ex=V((32, L, L), bf16), ld=V((48, L), bf16), q=V((4, 128, L), f32), qt=V((4, L, L), bf16),
        hx=V((16, C), bf16), hb=V((16, L), bf16), xp=V((4, L + 8, L), f32), bp=V((L + 8, L), f32),
        bslope=V((L, L), f32), bcv=V((L, L), f32), b2=V((L, L), bf16), c2=V((L, L), bf16),
        bt3=V((128, 768), bf16), ct3=V((128, 768), bf16), x=V((4, L, L), f32),
        slope=V((4, L, L), f32), xend=V((4, 2 * L, L), bf16), pst=V((8, 136, 128), f32),
        poth=V((8, 136, 128), f32), sc=V((L, L), f32), sct=V((L, L), f32), diag=V((L, 128), f32),
        sm=V((DENSE, L, 2 * L), bf16), smt=V((DENSE, L, 2 * L), bf16),
        wm=V((WIDE, 128, L), bf16), wmt=V((WIDE, 128, L), bf16), wx=V((WIDE, 4, L, L), bf16),
        wds=V((128, 128), f32), bgw=V((L, 128), f32), wg=V((WIDE, 4, L, L), bf16),
        ef=V((DENSE, 4, L, L), f32), we=V((WIDE, 4, 128, L), f32),
        wa=V((WIDE, 4, 128, L), f32), ga2=V((DENSE, 4, 2 * L, L), bf16), acc=V((4, L, L), f32),
        xe=V((DENSE, 4, 2 * L, L), bf16), ps=V((4, 136, 128), f32), xr=V((4, 136, 128), f32),
        ff=V((nf - 1, 2, 4, 128, 128), f32), cf=V((8, 8, 128), f32), df=V((8, 8, 128), f32),
        zs=V((nz, 136, 128), f32), zr=V((nz, 136, 128), f32), fb=V((2, 128, 128), f32),
        bx=V((4, 8, 128), f32), befs=V((nz, 8, 128), f32), fst=V((nz, 4, 128, 128), f32),
        fhl=V((nf, 4, L, L), bf16), st=V((2, L, 128), f32), gact=V((4, L, L), f32),
        g=V((4, L, L), f32), sts=V((8, L), f32), str=V((max(Y - 1, 1), 8, L), f32),
        inv=V((L, 128), f32), kk=V((L, 128), f32), gf=V((nf, 8, 128, 128), f32),
        go=V((nf - 1, 4, 128, 128), f32), ga=V((nf - 1, 4, 128, 128), f32),
        gx=V((nf - 1, 4, 128, 128), f32), g0r=V((8, 128, 128), f32), ds=V((L, L), f32),
        dsk=V((L, L), f32), cg=V((L, 128), f32), dv=V((L, 128), f32), dx=V((4, L, L), f32),
        dzs=V((nz, 128, 128), f32), dzr=V((nz, 128, 128), f32), dcur=V((128, 128), f32),
        dps=V((4, 128, 128), f32), dph=V((8, 128, 128), f32), bce=V((ny + 1, L, L), f32),
        bcer=V((max(ny, 1), L, L), f32), bl=V((ny + 1, L, 128), f32),
        blr=V((max(ny, 1), L, 128), f32), bs=V((ny + 1, 8, 128), f32), bsr=V((max(ny, 1), 8, 128), f32),
        nbs=V((8, L), f32), nbe=V((8, L), f32), hxs=V((8, C), f32), hxr=V((8, C), f32),
        ssem=pltpu.SemaphoreType.DMA((96,)), rsem=pltpu.SemaphoreType.DMA((96,)),
    )

    def per_device(x_raw, bc_raw, gate_raw, log_decay, level_weights, conv_x, conv_bc, gain, og):
        spec = pl.BlockSpec(memory_space=pltpu.VMEM)
        return pl.pallas_call(
            functools.partial(kernel, Z, Y, list(shapes)),
            out_shape=(
                jax.ShapeDtypeStruct((L, C), bf16),
                jax.ShapeDtypeStruct((L, C), bf16),
                jax.ShapeDtypeStruct((L, L), bf16),
            ),
            in_specs=[spec] * 9,
            out_specs=(spec,) * 3,
            scratch_shapes=list(shapes.values()),
            compiler_params=pltpu.CompilerParams(
                collective_id=0, has_side_effects=True, vmem_limit_bytes=67043328
            ),
        )(
            x_raw, bc_raw, gate_raw, og, log_decay, level_weights, conv_x, conv_bc,
            gain.reshape(1, C),
        )

    in_specs = (
        P("ctx", "head"), P("ctx", None), P("ctx", "head"), P("head", "ctx"),
        P(None, "head", "ctx"), P(None, "head"), P(), P("head"), P("ctx", "head"),
    )
    out_specs = (P("ctx", "head"), P("ctx", "head"), P("ctx", None))
    return jax.shard_map(
        per_device, mesh=mesh, in_specs=in_specs, out_specs=out_specs, check_vma=False
    )
```

```python
import functools

import jax
import jax.numpy as jnp
from jax import lax
from jax.experimental import pallas as pl
from jax.experimental.pallas import tpu as pltpu
from jax.sharding import PartitionSpec as P

MESH = pl.DeviceIdType.MESH
f32 = jnp.float32
bf16 = jnp.bfloat16
L = 256
C = 1024
INNER = 4096
EPS = 1e-05
LEV = 8
DENSE = 4
WIDE = LEV - DENSE


def split(v):
    hi = v.astype(bf16)
    return hi, (v - hi.astype(f32)).astype(bf16)


def mm(a, b):
    return jnp.dot(a, b, preferred_element_type=f32)


def mt(a, b):
    return lax.dot_general(a, b, (((1,), (1,)), ((), ())), preferred_element_type=f32)


def cat(parts, axis):
    return jnp.concatenate(parts, axis=axis)


def mm3(ah, al, bh, bl):
    return mm(cat([ah, ah, al], 1), cat([bh, bl, bh], 0))


def mt3(ah, al, bh, bl):
    return mt(cat([ah, ah, al], 1), cat([bh, bl, bh], 1))


def loop(n, fn, unroll=1):
    def step(i, carry):
        for t in range(unroll):
            fn(i * unroll + t)
        return carry

    lax.fori_loop(0, n // unroll, step, 0)


def sigmoid(v):
    return 1.0 / (1.0 + jnp.exp(-v))


def kernel(
    Z, Y, names,
    x_ref, bc_ref, gate_ref, og_ref, ld_ref, lw_ref, tx_ref, tb_ref, gain_ref,
    out_ref, xg_ref, bg_ref, *scratch,
):
    r = dict(zip(names, scratch))
    nz = Z.bit_length() - 1
    nctx = Z * 8
    nf = 3 + nz
    ctx = lax.axis_index("ctx")
    hd = lax.axis_index("head")
    core = ctx % 2
    xx = (ctx // 2) % 4
    zz = ctx // 8
    core_f = core.astype(f32)
    ssem, rsem = r["ssem"], r["rsem"]
    ids = {}

    def rc(key, src, dst, dev):
        i = ids.setdefault(key, len(ids))
        return pltpu.make_async_remote_copy(
            src_ref=src, dst_ref=dst, send_sem=ssem.at[i], recv_sem=rsem.at[i],
            device_id=dev, device_id_type=MESH,
        )

    def at_x(q):
        return (zz * 8 + q * 2 + core, hd)

    def mirror(m):
        w = 2 ** (m + 1)
        return ((zz // w) * w + (w - 1) - zz % w) * 8 + xx * 2 + core

    def zbit(m):
        return (zz // 2**m) % 2

    other = (ctx + 1 - 2 * core, hd)
    following = ((ctx + 1) % nctx, hd)
    preceding = ((ctx + nctx - 1) % nctx, hd)

    def cbit(l):
        if l == 1:
            return xx % 2
        if l == 2:
            return xx // 2
        return zbit(l - 3)

    peers = [other, following, preceding]
    peers += [at_x((xx + d) % 4) for d in (1, 2, 3)]
    peers += [(mirror(m), hd) for m in range(nz)]
    peers += [(ctx, (hd + d) % Y) for d in range(1, Y)]
    yp = []
    w = 2
    while w <= Y:
        yp.append((ctx, (hd // w) * w + (w - 1) - hd % w))
        w *= 2
    barrier = pltpu.get_barrier_semaphore()
    for dev in peers:
        pl.semaphore_signal(barrier, inc=1, device_id=dev, device_id_type=MESH)

    pend = []

    def cols(j):
        return pl.ds(pl.multiple_of(j * 256, 256), 256)

    row = lax.broadcasted_iota(jnp.int32, (L, L), 0)
    col = lax.broadcasted_iota(jnp.int32, (L, L), 1)
    dist = row ^ col
    r["zle"][...] = jnp.where(row <= col, dist, 4096)
    r["zgt"][...] = jnp.where(row > col, dist, 4096)
    r["zlt"][...] = jnp.where(row < col, dist, 4096)

    def make_ex(o):
        a = lax.broadcasted_iota(jnp.int32, (L, L), 0) % 128
        b = lax.broadcasted_iota(jnp.int32, (L, L), 1) // 64
        r["ex"][o] = jnp.where(a == b + 4 * o, 1.0, 0.0).astype(bf16)

    loop(8, lambda i: make_ex(i + 24))
    ld = ld_ref[...]
    l0 = ld.astype(bf16)
    rest = ld - l0.astype(f32)
    l1 = rest.astype(bf16)
    l2 = (rest - l1.astype(f32)).astype(bf16)
    r["ld"][...] = cat([l0, l1, l2], 0)
    q = r["q"]

    def sums(mask):
        t = mm(r["ld"][...], jnp.where(mask, 1.0, 0.0).astype(bf16))
        return t[0:16] + t[16:32] + t[32:48]

    up = sums(r["zle"][...] < L)
    dn = sums(r["zgt"][...] < L)
    eup = jnp.exp(up)
    for l in range(nf):
        q[2, l * 16 : l * 16 + 16, :] = lw_ref[min(LEV + 1 + l, 15)] * eup
    for l in range(nf, 6):
        q[2, l * 16 : l * 16 + 16, :] = jnp.zeros((16, L), f32)
    q[2, 96:112, :] = jnp.exp(dn)
    q[2, 112:128, :] = jnp.broadcast_to(eup[:, L - 1 : L], (16, L))
    def pack(g):
        hi, lo = split(q[g].T)
        r["qt"][g, :, 0:128] = hi
        r["qt"][g, :, 128:256] = lo

    pack(2)

    def spread(g, i, j):
        return mm(r["qt"][g], r["ex"][i * 4 + j])

    pl.semaphore_wait(barrier, len(peers))
    hx = rc("hx", x_ref.at[L - 16 : L], r["hx"], following)
    hb = rc("hb", bc_ref.at[L - 16 : L], r["hb"], following)
    hx.start()
    hb.start()
    pend += [hx, hb]
    xp, bp = r["xp"], r["bp"]

    def widen(j):
        xp[j, 8 : L + 8, :] = x_ref[:, cols(j)].astype(f32)

    loop(4, widen)
    bp[8 : L + 8, :] = bc_ref[...].astype(f32)
    def pre_act(j, lo, hi):
        pre = tx_ref[0:1, cols(j)] * xp[j, lo + 5 : hi + 5, :]
        for k in range(1, 4):
            pre = pre + tx_ref[k : k + 1, cols(j)] * xp[j, lo + 5 + k : hi + 5 + k, :]
        sig = sigmoid(pre)
        r["x"][j, lo:hi] = pre * sig
        r["slope"][j, lo:hi] = sig * (1.0 + pre * (1.0 - sig))

    loop(4, lambda j: pre_act(j, 8, L))
    has_prev = jnp.where(ctx > 0, 1.0, 0.0).astype(f32)
    hx.wait_recv()
    hb.wait_recv()
    for j in range(4):
        xp[j, 0:8, :] = r["hx"][:, j * 256 : j * 256 + 256].astype(f32)[8:16] * has_prev
    bp[0:8, :] = r["hb"][...].astype(f32)[8:16] * has_prev

    for j in range(4):
        pre_act(j, 0, 8)
    bpre = tb_ref[0:1] * bp[5 : L + 5, :]
    for k in range(1, 4):
        bpre = bpre + tb_ref[k : k + 1] * bp[5 + k : L + 5 + k, :]
    bsig = sigmoid(bpre)
    r["bslope"][...] = bsig * (1.0 + bpre * (1.0 - bsig))
    nbs = rc("nbs", r["bslope"].at[0:8], r["nbs"], preceding)
    nbs.start()
    pend.append(nbs)
    bcv = bpre * bsig
    r["bcv"][...] = bcv
    b = bcv[:, 0:128]
    c = bcv[:, 128:256]
    bh, bl = split(b)
    ch, cl = split(c)
    bth, btl = split(b.T)
    cth, ctl = split(c.T)
    r["b2"][...] = cat([bh, bl], 1)
    r["c2"][...] = cat([ch, cl], 1)
    r["bt3"][...] = cat([bth, bth, btl], 1)
    r["ct3"][...] = cat([cth, cth, ctl], 1)
    pst = r["pst"]

    def end_state(j):
        hi, lo = split(r["x"][j] * spread(2, 6, j))
        r["xend"][j, 0:L] = hi
        r["xend"][j, L : 2 * L] = lo
        s = mm(r["bt3"][...], cat([hi, lo, hi], 0))
        d = mm(r["qt"][2, 0:16, :], r["ex"][28 + j])[0:8]
        for h in range(2):
            pst[2 * j + h, 0:128] = s[:, h * 128 : h * 128 + 128]
            pst[2 * j + h, 128:136] = d[:, h * 128 : h * 128 + 128]

    loop(4, end_state, 2)

    p0 = rc("p0", pst, r["poth"], other)
    p0.start()
    pend.append(p0)
    poth = r["poth"]

    sc = mt3(ch, cl, bh, bl)
    sct = mt3(bh, bl, ch, cl)
    r["sc"][...] = sc
    r["sct"][...] = sct
    diag = jnp.sum(c * b, axis=1, keepdims=True)
    r["diag"][...] = jnp.broadcast_to(diag, (L, 128))

    def level_masks(k):
        th = lax.shift_left(jnp.int32(1), k)
        z = r["zgt"][...]
        hi, lo = split(jnp.where((z >= th) & (z < 2 * th), r["sc"][...], 0.0))
        r["sm"][k, :, 0:L] = hi
        r["sm"][k, :, L : 2 * L] = lo
        z = r["zlt"][...]
        hi, lo = split(jnp.where((z >= th) & (z < 2 * th), r["sct"][...], 0.0))
        r["smt"][k, :, 0:L] = hi
        r["smt"][k, :, L : 2 * L] = lo

    loop(DENSE, level_masks)

    def low(k, get):
        h = 2**k
        return cat([get(s, s + h) for s in range(0, L, 2 * h)], 0)

    def upp(k, get):
        h = 2**k
        return cat([get(s + h, s + 2 * h) for s in range(0, L, 2 * h)], 0)

    def same(k):
        u = lax.broadcasted_iota(jnp.int32, (128, 128), 0) // 2**k
        v = lax.broadcasted_iota(jnp.int32, (128, 128), 1) // 2**k
        return u == v

    for k in range(DENSE, LEV):
        cu = upp(k, lambda a, b: r["c2"][a:b])
        bw = low(k, lambda a, b: r["b2"][a:b])
        cuh, cul, bwh, bwl = cu[:, 0:128], cu[:, 128:256], bw[:, 0:128], bw[:, 128:256]
        w = k - DENSE
        hi, lo = split(jnp.where(same(k), mt3(cuh, cul, bwh, bwl), 0.0))
        r["wm"][w, :, 0:128] = hi
        r["wm"][w, :, 128:256] = lo
        hi, lo = split(jnp.where(same(k), mt3(bwh, bwl, cuh, cul), 0.0))
        r["wmt"][w, :, 0:128] = hi
        r["wmt"][w, :, 128:256] = lo

    def near(j):
        dg = r["diag"][...]
        r["acc"][j] = spread(3, 0, j) * (cat([dg, dg], 1) * r["x"][j])

        def level(k):
            e = spread(1, k, j)
            r["ef"][k, j] = e
            hi, lo = split(r["x"][j] * e)
            r["xe"][k, j, 0:L] = hi
            r["xe"][k, j, L : 2 * L] = lo
            m = r["sm"][k]
            y = mm(cat([m[:, 0:L], m], 1), cat([hi, lo, hi], 0))
            a = spread(0, k, j)
            r["acc"][j] = r["acc"][j] + a * y

        loop(DENSE, level, 2)
        for k in range(DENSE, LEV):
            w, h = k - DENSE, 2**k
            e = mm(low(k, lambda a, b: r["qt"][1, a:b]), r["ex"][k * 4 + j])
            r["we"][w, j] = e
            hi, lo = split(low(k, lambda a, b: r["x"][j, a:b]) * e)
            r["wx"][w, j, 0:128] = hi
            r["wx"][w, j, 128:256] = lo
            m = r["wm"][w]
            y = mm(cat([m[:, 0:128], m], 1), cat([hi, lo, hi], 0))
            a = mm(upp(k, lambda a, b: r["qt"][0, a:b]), r["ex"][k * 4 + j])
            r["wa"][w, j] = a
            y = y * a
            for i in range(128 // h):
                at = slice((2 * i + 1) * h, (2 * i + 2) * h)
                r["acc"][j, at] = r["acc"][j, at] + y[i * h : (i + 1) * h]

    p0.wait_recv()
    ps, xr, ff = r["ps"], r["xr"], r["ff"]
    for h in range(4):
        own = pst[core * 4 + h]
        oth = poth[core * 4 + h]
        lo = jnp.where(core == 0, own, oth)
        hi = jnp.where(core == 0, oth, own)
        ps[h, 0:128] = lo[0:128] * hi[128:129] + hi[0:128]
        ps[h, 128:136] = lo[128:136] * hi[128:136]
    xr[xx] = ps[xx]
    for p in range(8):
        dd = poth[p, 128:136]
        r["cf"][p] = jnp.where(core == 1, dd, 1.0)
        r["df"][p] = jnp.where(core == 0, dd, 1.0)
    xs = []
    for d in (1, 2, 3):
        to = (xx + d) % 4
        xs.append(rc(("xs", d), ps.at[to], xr.at[xx], at_x(to)))
        xs[-1].start()
    pend += xs

    loop(24, make_ex)
    def coefs(k):
        th = lax.shift_left(jnp.int32(1), k)
        up = sums(r["zle"][...] < th)
        dn = sums(r["zgt"][...] < th)
        at = pl.ds(pl.multiple_of(k * 16, 16), 16)
        q[0, at, :] = lw_ref[k + 1] * jnp.exp(up)
        q[1, at, :] = jnp.exp(dn)

    loop(LEV, coefs)
    q[3] = jnp.zeros((128, L), f32)
    q[3, 0:16, :] = lw_ref[0]
    for g in (0, 1, 3):
        pack(g)

    near(0)
    near(1)

    for cp in xs:
        cp.wait_recv()
    dec = [xr[i, 128:129] for i in range(4)]
    b01 = xr[0, 0:128] * dec[1] + xr[1, 0:128]
    b23 = xr[2, 0:128] * dec[3] + xr[3, 0:128]
    d01 = dec[0] * dec[1]
    d23 = dec[2] * dec[3]
    zs, zr, fb, bx, befs = r["zs"], r["zr"], r["fb"], r["bx"], r["befs"]
    zs[0, 0:128] = b01 * d23 + b23
    zs[0, 128:136] = jnp.broadcast_to(d01 * d23, (8, 128))
    fb[0] = b01
    fb[1] = b01 * dec[2]
    bx[0] = jnp.ones((8, 128), f32)
    bx[1] = jnp.broadcast_to(dec[0], (8, 128))
    bx[2] = jnp.broadcast_to(d01, (8, 128))
    bx[3] = jnp.broadcast_to(d01 * dec[2], (8, 128))
    befs[0] = jnp.ones((8, 128), f32)

    def z_copy(m):
        return rc(("z", m), zs.at[m], zr.at[m], (mirror(m), hd))

    def z_start(m):
        if m < nz - 1:
            z_copy(m).start()
        else:
            @pl.when(zbit(m) == 0)
            def _():
                z_copy(m).start()

    def f_copy(l, d):
        to = (xx + d) % 4
        if l == 1:
            src = xr.at[(to + 3) % 4, 0:128]
        elif l == 2:
            src = fb.at[to % 2]
        else:
            src = r["fst"].at[l - 3, to]
        return rc(("f", l, d), src, ff.at[l - 1, core, xx], at_x(to))

    def to_bit(l, d):
        to = (xx + d) % 4
        return to % 2 if l == 1 else to // 2 if l == 2 else zbit(l - 3)

    def from_bit(l, d):
        fr = (xx + 4 - d) % 4
        return fr % 2 if l == 1 else fr // 2 if l == 2 else zbit(l - 3)

    def f_send(l):
        for d in (1, 2, 3):
            @pl.when(to_bit(l, d) == 1)
            def _():
                f_copy(l, d).start()

    def fo_copy(l):
        return rc(("fo", l), ff.at[l - 1, core], ff.at[l - 1, core], other)

    def f_relay(l):
        @pl.when(cbit(l) == 1)
        def _():
            for d in (1, 2, 3):
                f_copy(l, d).wait_recv()
            fo_copy(l).start()

    z_start(0)

    @pl.when(xx % 2 == 1)
    def _():
        ff[0, core, xx] = xr[(xx + 3) % 4, 0:128]

    @pl.when(xx // 2 == 1)
    def _():
        ff[1, core, xx] = fb[xx % 2]

    f_send(2)
    f_send(1)

    def z_done(m):
        up = zbit(m)

        @pl.when(up == 1)
        def _():
            z_copy(m).wait_recv()
            f = zr[m, 0:128] * befs[m, 0:1]
            for i in range(4):
                r["fst"][m, i] = f * bx[i, 0:1]
            ff[2 + m, core, xx] = f * bx[xx, 0:1]
            if m < nz - 1:
                zs[m + 1, 0:128] = zr[m, 0:128] * zs[m, 128:129] + zs[m, 0:128]
                befs[m + 1] = befs[m] * zr[m, 128:136]

        if m < nz - 1:
            @pl.when(up == 0)
            def _():
                z_copy(m).wait_recv()
                zs[m + 1, 0:128] = zs[m, 0:128] * zr[m, 128:129] + zr[m, 0:128]
                befs[m + 1] = befs[m]

            zs[m + 1, 128:136] = zs[m, 128:136] * zr[m, 128:136]
            z_start(m + 1)
        f_send(3 + m)

    near(2)
    z_done(0)
    near(3)
    f_relay(2)
    f_relay(1)

    fhl = r["fhl"]

    def inter(l, j, f):
        hi, lo = split(f)
        fhl[l, j, 0:128] = hi
        fhl[l, j, 128:256] = lo
        c2 = r["c2"][...]
        y = mm(cat([c2[:, 0:128], c2[:, 0:128]], 1), cat([hi, lo], 0)) + mm(c2[:, 128:256], hi)
        r["acc"][j] = r["acc"][j] + spread(2, l, j) * y

    @pl.when(core == 1)
    def _():
        def f0(j):
            inter(0, j, cat([poth[2 * j, 0:128], poth[2 * j + 1, 0:128]], 1))

        loop(4, f0)

    def far(l):
        @pl.when(cbit(l) == 1)
        def _():
            fo_copy(l).wait_recv()

            def one(j):
                parts = [
                    ff[l - 1, j // 2, (j % 2) * 2 + h] * r["cf"][2 * j + h, 0:1] for h in range(2)
                ]
                inter(l, j, cat(parts, 1))

            loop(4, one, 4)

    if nz > 1:
        z_done(1)
    f_relay(3)
    far(2)
    far(1)

    def gate_first(j):
        g = gate_ref[:, cols(j)].astype(f32)
        r["gact"][j] = g * sigmoid(g)
        r["g"][j] = gain_ref[:, cols(j)] * og_ref[:, cols(j)].astype(f32)

    loop(4, gate_first)
    for m in range(2, nz):
        z_done(m)
        if m == 2:
            f_relay(4)
    far(3)
    for l in range(4, nf):
        if l > 4 or nz <= 2:
            f_relay(l)
        far(l)

    r["st"][...] = jnp.zeros((2, L, 128), f32)

    def gated(j):
        mixed = r["acc"][j] * r["gact"][j]
        r["acc"][j] = mixed
        sg = r["g"][j]
        sq = mixed * mixed
        cr = sg * mixed
        r["st"][0] = r["st"][0] + (sq[:, 0:128] + sq[:, 128:256])
        r["st"][1] = r["st"][1] + (cr[:, 0:128] + cr[:, 128:256])

    loop(4, gated)
    s0 = jnp.sum(r["st"][0], axis=1, keepdims=True)
    s1 = jnp.sum(r["st"][1], axis=1, keepdims=True)
    lane = lax.broadcasted_iota(jnp.int32, (L, 128), 1)
    both = jnp.where(lane == 0, s0, s1)
    r["sts"][...] = both.T[0:8]
    ys = []
    for d in range(1, Y):
        ys.append(rc(("st", d), r["sts"], r["str"].at[d - 1], (ctx, (hd + d) % Y)))
        ys[-1].start()
    pend += ys
    tot = r["sts"][...]
    for d in range(1, Y):
        ys[d - 1].wait_recv()
        tot = tot + r["str"][d - 1]
    inv_row = lax.rsqrt(tot[0:1] / INNER + EPS)
    k_row = inv_row * inv_row * inv_row * (tot[1:2] / INNER)
    r["inv"][...] = jnp.broadcast_to(inv_row, (128, L)).T
    r["kk"][...] = jnp.broadcast_to(k_row, (128, L)).T

    def normed(j):
        inv = cat([r["inv"][...]] * 2, 1)
        kk = cat([r["kk"][...]] * 2, 1)
        mixed = r["acc"][j]
        out_ref[:, cols(j)] = (gain_ref[:, cols(j)] * mixed * inv).astype(bf16)
        r["g"][j] = (r["g"][j] * inv - mixed * kk) * r["gact"][j]

    loop(4, normed)

    gf, go, ga_, gx = r["gf"], r["go"], r["ga"], r["gx"]

    def go_copy(l):
        return rc(("go", l), gf.at[l, pl.ds((1 - core) * 4, 4)], go.at[l - 1], other)

    def far_grad(l):
        def one(j):
            hi, lo = split(r["g"][j] * spread(2, l, j))
            s = mm(r["ct3"][...], cat([hi, lo, hi], 0))
            r["cg"][...] = r["cg"][...] + mt3(hi, lo, fhl[l, j, 0:128], fhl[l, j, 128:256])
            for h in range(2):
                piece = s[:, h * 128 : h * 128 + 128]
                if l > 0:
                    piece = piece * r["cf"][2 * j + h, 0:1]
                gf[l, 2 * j + h] = piece

        loop(4, one, 4)

    def g0_copy():
        return rc("g0", gf.at[0], r["g0r"], other)

    def gx_copy(l, d):
        to = (xx + d) % 4
        return rc(("gx", l, d), ga_.at[l - 1, to], gx.at[l - 1, xx], at_x(to))

    def g_pair(l):
        @pl.when(cbit(l) == 1)
        def _():
            go_copy(l).wait_recv()
            for h in range(4):
                ga_[l - 1, h] = gf[l, core * 4 + h] + go[l - 1, h]
            for d in (1, 2, 3):
                gx_copy(l, d).start()
            gx[l - 1, xx] = ga_[l - 1, xx]

    def fg(l):
        @pl.when((core if l == 0 else cbit(l)) == 1)
        def _():
            far_grad(l)
            (go_copy(l) if l else g0_copy()).start()

    r["ds"][...] = jnp.zeros((L, L), f32)
    r["cg"][...] = jnp.zeros((L, 128), f32)
    r["bgw"][...] = jnp.zeros((L, 128), f32)

    fg(nf - 1)
    for l in range(nf - 2, -1, -1):
        fg(l)
        g_pair(l + 1)

    def first_dx(j):
        dg = r["diag"][...]
        gw = r["g"][j] * spread(3, 0, j)
        r["dx"][j] = gw * cat([dg, dg], 1)
        pr = gw * r["x"][j]
        r["dv"][...] = r["dv"][...] + (pr[:, 0:128] + pr[:, 128:256])

    r["dv"][...] = jnp.zeros((L, 128), f32)
    loop(4, first_dx)

    def near_ds(k):
        r["dsk"][...] = jnp.zeros((L, L), f32)

        def one(j):
            hi, lo = split(r["g"][j] * spread(0, k, j))
            r["ga2"][k, j, 0:L] = hi
            r["ga2"][k, j, L : 2 * L] = lo
            eh = r["xe"][k, j, 0:L]
            el = r["xe"][k, j, L : 2 * L]
            r["dsk"][...] = r["dsk"][...] + mt3(hi, lo, eh, el)

        loop(4, one, 4)
        th = lax.shift_left(jnp.int32(1), k)
        z = r["zgt"][...]
        r["ds"][...] = r["ds"][...] + jnp.where((z >= th) & (z < 2 * th), r["dsk"][...], 0.0)

    def near_dx(k):
        def one(j):
            hi = r["ga2"][k, j, 0:L]
            lo = r["ga2"][k, j, L : 2 * L]
            m = r["smt"][k]
            y = mm(cat([m[:, 0:L], m], 1), cat([hi, lo, hi], 0))
            r["dx"][j] = r["dx"][j] + r["ef"][k, j] * y

        loop(4, one, 4)

    def wide_ds(k):
        w, h = k - DENSE, 2**k
        r["wds"][...] = jnp.zeros((128, 128), f32)

        def one(j):
            hi, lo = split(upp(k, lambda a, b: r["g"][j, a:b]) * r["wa"][w, j])
            r["wg"][w, j, 0:128] = hi
            r["wg"][w, j, 128:256] = lo
            eh = r["wx"][w, j, 0:128]
            el = r["wx"][w, j, 128:256]
            r["wds"][...] = r["wds"][...] + mt3(hi, lo, eh, el)

        loop(4, one, 4)
        d = jnp.where(same(k), r["wds"][...], 0.0)
        dh, dl = split(d)
        th, tl = split(d.T)
        cu = upp(k, lambda a, b: r["c2"][a:b])
        bw = low(k, lambda a, b: r["b2"][a:b])
        cg = mm3(dh, dl, bw[:, 0:128], bw[:, 128:256])
        bg = mm3(th, tl, cu[:, 0:128], cu[:, 128:256])
        for i in range(128 // h):
            at = slice(2 * i * h, (2 * i + 1) * h)
            r["bgw"][at] = r["bgw"][at] + bg[i * h : (i + 1) * h]
            at = slice((2 * i + 1) * h, (2 * i + 2) * h)
            r["cg"][at] = r["cg"][at] + cg[i * h : (i + 1) * h]

    def wide_dx(k):
        w, h = k - DENSE, 2**k

        def one(j):
            hi = r["wg"][w, j, 0:128]
            lo = r["wg"][w, j, 128:256]
            m = r["wmt"][w]
            y = mm(cat([m[:, 0:128], m], 1), cat([hi, lo, hi], 0)) * r["we"][w, j]
            for i in range(128 // h):
                at = slice(2 * i * h, (2 * i + 1) * h)
                r["dx"][j, at] = r["dx"][j, at] + y[i * h : (i + 1) * h]

        loop(4, one, 4)

    def dense(fn, lo, hi):
        def step(k, carry):
            fn(k)
            return carry

        lax.fori_loop(lo, hi, step, 0)

    dzs, dzr, dcur = r["dzs"], r["dzr"], r["dcur"]

    def dz_copy(m):
        return rc(("dz", m), dzs.at[m], dzr.at[m], (mirror(m), hd))

    def dz_start(m):
        last = m == nz - 1

        @pl.when(zbit(m) == 1)
        def _():
            for d in (1, 2, 3):
                gx_copy(3 + m, d).wait_recv()
            f = gx[2 + m, 0]
            for i in range(1, 4):
                f = f + gx[2 + m, i] * bx[i, 0:1]
            f = f * befs[m, 0:1]
            if not last:
                f = f + dcur[...] * zs[m, 128:129]
            dzs[m] = f
            dz_copy(m).start()

        if not last:
            @pl.when(zbit(m) == 0)
            def _():
                dzs[m] = dcur[...]
                dz_copy(m).start()

    def dz_done(m):
        if m == nz - 1:
            @pl.when(zbit(m) == 1)
            def _():
                dcur[...] = jnp.zeros((128, 128), f32)

            @pl.when(zbit(m) == 0)
            def _():
                dz_copy(m).wait_recv()
                dcur[...] = dzr[m]
        else:
            dz_copy(m).wait_recv()

            @pl.when(zbit(m) == 1)
            def _():
                dcur[...] = dcur[...] + dzr[m]

            @pl.when(zbit(m) == 0)
            def _():
                dcur[...] = dcur[...] * zr[m, 128:129] + dzr[m]

    dz_start(nz - 1)
    dense(near_ds, 0, DENSE)
    if nz > 1:
        dz_done(nz - 1)
        dz_start(nz - 2)
    for k in range(DENSE, LEV):
        wide_ds(k)
    if nz == 1:
        dz_done(0)
    ds = r["ds"][...]
    dsh, dsl = split(ds)
    dth, dtl = split(ds.T)
    b2 = r["b2"][...]
    c2 = r["c2"][...]
    dv = jnp.sum(r["dv"][...], axis=1, keepdims=True)
    cg = r["cg"][...] + mm3(dsh, dsl, b2[:, 0:128], b2[:, 128:256]) + dv * r["bcv"][:, 0:128]
    bg = r["bgw"][...] + mm3(dth, dtl, c2[:, 0:128], c2[:, 128:256]) + dv * r["bcv"][:, 128:256]
    r["bce"][0, :, 0:128] = bg
    r["bce"][0, :, 128:256] = cg
    def y_start(key, src, dst, step):
        cp = rc((key, step), src.at[step], dst.at[step], yp[step])
        cp.start()
        pend.append(cp)
        return cp

    def y_sum(key, src, dst, step):
        rc((key, step), src.at[step], dst.at[step], yp[step]).wait_recv()
        src[step + 1] = src[step] + dst[step]

    ny = len(yp)
    if ny:
        y_start("be", r["bce"], r["bcer"], 0)

    for m in range(nz - 2, -1, -1):
        dz_done(m)
        if m:
            dz_start(m - 1)
        if m == nz - 2:
            dense(near_dx, 0, 2)

    dps, dph = r["dps"], r["dph"]
    for l in (1, 2):
        for d in (1, 2, 3):
            @pl.when(from_bit(l, d) == 1)
            def _():
                gx_copy(l, d).wait_recv()

    dt = dcur[...]
    dec = [xr[i, 128:129] for i in range(4)]
    d01 = dt * (dec[2] * dec[3]) + (gx[1, 2] + gx[1, 3] * dec[2])
    dps[0] = d01 * dec[1] + gx[0, 1]
    dps[1] = d01
    dps[2] = dt * dec[3] + gx[0, 3]
    dps[3] = dt
    dpc = []
    for d in (1, 2, 3):
        to = (xx + d) % 4
        dpc.append(rc(("dp", d), dps.at[to], dph.at[core * 4 + xx], at_x(to)))
        dpc[-1].start()
    pend += dpc
    dph[core * 4 + xx] = dps[xx]

    dense(near_dx, 2 if nz > 1 else 0, DENSE)
    wide_dx(DENSE)
    if ny > 1:
        y_sum("be", r["bce"], r["bcer"], 0)
        y_start("be", r["bce"], r["bcer"], 1)
    for k in range(DENSE + 1, LEV):
        wide_dx(k)

    for cp in dpc:
        cp.wait_recv()
    half = pl.ds(core * 4, 4)
    dpo = rc("dpo", dph.at[half], dph.at[half], other)
    dpo.start()

    dpo.wait()

    @pl.when(core == 0)
    def _():
        g0_copy().wait_recv()
        for p in range(8):
            dph[p] = dph[p] * r["df"][p, 0:1] + r["g0r"][p]

    r["bl"][0] = jnp.zeros((L, 128), f32)
    xsl = r["xp"]

    def last_dx(j):
        hi, lo = split(cat([dph[2 * j], dph[2 * j + 1]], 1))
        r["bl"][0] = r["bl"][0] + mt3(r["xend"][j, 0:L], r["xend"][j, L : 2 * L], hi, lo)
        b2 = r["b2"][...]
        y = mm(cat([b2[:, 0:128], b2[:, 0:128]], 1), cat([hi, lo], 0)) + mm(b2[:, 128:256], hi)
        dx = r["dx"][j] + spread(2, 6, j) * y
        sl = dx * r["slope"][j]
        xsl[j, 0:L] = sl
        r["hxs"][:, cols(j)] = sl[0:8]

    loop(4, last_dx)
    nx = rc("nx", r["hxs"], r["hxr"], preceding)
    nx.start()
    n8 = rc("n8", r["bl"].at[0, 0:8], r["bs"].at[0], preceding)
    n8.start()
    pend += [nx, n8]
    if ny:
        y_start("bl", r["bl"], r["blr"], 0)
    for i in range(min(1, ny - 1), ny):
        y_sum("be", r["bce"], r["bcer"], i)
        if i < ny - 1:
            y_start("be", r["bce"], r["bcer"], i + 1)
    n8.wait_recv()
    if ny:
        y_start("bs", r["bs"], r["bsr"], 0)
    nbe = rc("nbe", r["bce"].at[ny, 0:8], r["nbe"], preceding)
    nbe.start()
    pend.append(nbe)
    has_next = jnp.where(ctx < nctx - 1, 1.0, 0.0).astype(f32)

    nx.wait_recv()
    for j in range(4):
        xsl[j, L : L + 8] = r["hxr"][:, j * 256 : j * 256 + 256] * has_next

    def conv_back(j):
        v = tx_ref[3:4, cols(j)] * xsl[j, 0:L]
        for k in range(3):
            v = v + tx_ref[k : k + 1, cols(j)] * xsl[j, 3 - k : L + 3 - k]
        xg_ref[:, cols(j)] = v.astype(bf16)

    loop(4, conv_back)
    for i in range(ny):
        y_sum("bl", r["bl"], r["blr"], i)
        y_sum("bs", r["bs"], r["bsr"], i)
        if i < ny - 1:
            y_start("bl", r["bl"], r["blr"], i + 1)
            y_start("bs", r["bs"], r["bsr"], i + 1)
    total = r["bce"][ny]
    bp[0:L, :] = cat([total[:, 0:128] + r["bl"][ny], total[:, 128:256]], 1) * r["bslope"][...]
    nbs.wait_recv()
    nbe.wait_recv()
    total = r["nbe"][...]
    rows = cat([total[:, 0:128] + r["bs"][ny], total[:, 128:256]], 1)
    bp[L : L + 8, :] = rows * r["nbs"][...] * has_next
    v = tb_ref[3:4] * bp[0:L, :]
    for k in range(3):
        v = v + tb_ref[k : k + 1] * bp[3 - k : L + 3 - k, :]
    bg_ref[...] = v.astype(bf16)

    for cp in pend:
        cp.wait_send()
    for m in range(nz):
        if m < nz - 1:
            z_copy(m).wait_send()
            dz_copy(m).wait_send()
        else:
            @pl.when(zbit(m) == 0)
            def _():
                z_copy(m).wait_send()

            @pl.when(zbit(m) == 1)
            def _():
                dz_copy(m).wait_send()
    for l in range(1, nf):
        for d in (1, 2, 3):
            @pl.when(to_bit(l, d) == 1)
            def _():
                f_copy(l, d).wait_send()

        @pl.when(cbit(l) == 1)
        def _():
            fo_copy(l).wait_send()
            go_copy(l).wait_send()
            for d in (1, 2, 3):
                gx_copy(l, d).wait_send()

    @pl.when(core == 1)
    def _():
        g0_copy().wait_send()


def solution(mesh):
    nctx, Y = mesh.shape["ctx"], mesh.shape["head"]
    Z = nctx // 8
    nz = Z.bit_length() - 1
    nf = 3 + nz
    ny = Y.bit_length() - 1
    V = pltpu.VMEM
    shapes = dict(
        zle=V((L, L), jnp.int32), zgt=V((L, L), jnp.int32), zlt=V((L, L), jnp.int32),
        ex=V((32, L, L), bf16), ld=V((48, L), bf16), q=V((4, 128, L), f32), qt=V((4, L, L), bf16),
        hx=V((16, C), bf16), hb=V((16, L), bf16), xp=V((4, L + 8, L), f32), bp=V((L + 8, L), f32),
        bslope=V((L, L), f32), bcv=V((L, L), f32), b2=V((L, L), bf16), c2=V((L, L), bf16),
        bt3=V((128, 768), bf16), ct3=V((128, 768), bf16), x=V((4, L, L), f32),
        slope=V((4, L, L), f32), xend=V((4, 2 * L, L), bf16), pst=V((8, 136, 128), f32),
        poth=V((8, 136, 128), f32), sc=V((L, L), f32), sct=V((L, L), f32), diag=V((L, 128), f32),
        sm=V((DENSE, L, 2 * L), bf16), smt=V((DENSE, L, 2 * L), bf16),
        wm=V((WIDE, 128, L), bf16), wmt=V((WIDE, 128, L), bf16), wx=V((WIDE, 4, L, L), bf16),
        wds=V((128, 128), f32), bgw=V((L, 128), f32), wg=V((WIDE, 4, L, L), bf16),
        ef=V((DENSE, 4, L, L), f32), we=V((WIDE, 4, 128, L), f32),
        wa=V((WIDE, 4, 128, L), f32), ga2=V((DENSE, 4, 2 * L, L), bf16), acc=V((4, L, L), f32),
        xe=V((DENSE, 4, 2 * L, L), bf16), ps=V((4, 136, 128), f32), xr=V((4, 136, 128), f32),
        ff=V((nf - 1, 2, 4, 128, 128), f32), cf=V((8, 8, 128), f32), df=V((8, 8, 128), f32),
        zs=V((nz, 136, 128), f32), zr=V((nz, 136, 128), f32), fb=V((2, 128, 128), f32),
        bx=V((4, 8, 128), f32), befs=V((nz, 8, 128), f32), fst=V((nz, 4, 128, 128), f32),
        fhl=V((nf, 4, L, L), bf16), st=V((2, L, 128), f32), gact=V((4, L, L), f32),
        g=V((4, L, L), f32), sts=V((8, L), f32), str=V((max(Y - 1, 1), 8, L), f32),
        inv=V((L, 128), f32), kk=V((L, 128), f32), gf=V((nf, 8, 128, 128), f32),
        go=V((nf - 1, 4, 128, 128), f32), ga=V((nf - 1, 4, 128, 128), f32),
        gx=V((nf - 1, 4, 128, 128), f32), g0r=V((8, 128, 128), f32), ds=V((L, L), f32),
        dsk=V((L, L), f32), cg=V((L, 128), f32), dv=V((L, 128), f32), dx=V((4, L, L), f32),
        dzs=V((nz, 128, 128), f32), dzr=V((nz, 128, 128), f32), dcur=V((128, 128), f32),
        dps=V((4, 128, 128), f32), dph=V((8, 128, 128), f32), bce=V((ny + 1, L, L), f32),
        bcer=V((max(ny, 1), L, L), f32), bl=V((ny + 1, L, 128), f32),
        blr=V((max(ny, 1), L, 128), f32), bs=V((ny + 1, 8, 128), f32), bsr=V((max(ny, 1), 8, 128), f32),
        nbs=V((8, L), f32), nbe=V((8, L), f32), hxs=V((8, C), f32), hxr=V((8, C), f32),
        ssem=pltpu.SemaphoreType.DMA((96,)), rsem=pltpu.SemaphoreType.DMA((96,)),
    )

    def per_device(x_raw, bc_raw, gate_raw, log_decay, level_weights, conv_x, conv_bc, gain, og):
        spec = pl.BlockSpec(memory_space=pltpu.VMEM)
        return pl.pallas_call(
            functools.partial(kernel, Z, Y, list(shapes)),
            out_shape=(
                jax.ShapeDtypeStruct((L, C), bf16),
                jax.ShapeDtypeStruct((L, C), bf16),
                jax.ShapeDtypeStruct((L, L), bf16),
            ),
            in_specs=[spec] * 9,
            out_specs=(spec,) * 3,
            scratch_shapes=list(shapes.values()),
            compiler_params=pltpu.CompilerParams(
                collective_id=0, has_side_effects=True, vmem_limit_bytes=67043328
            ),
        )(
            x_raw, bc_raw, gate_raw, og, log_decay, level_weights, conv_x, conv_bc,
            gain.reshape(1, C),
        )

    in_specs = (
        P("ctx", "head"), P("ctx", None), P("ctx", "head"), P("head", "ctx"),
        P(None, "head", "ctx"), P(None, "head"), P(), P("head"), P("ctx", "head"),
    )
    out_specs = (P("ctx", "head"), P("ctx", "head"), P("ctx", None))
    return jax.shard_map(
        per_device, mesh=mesh, in_specs=in_specs, out_specs=out_specs, check_vma=False
    )
```
